128 devices in a mesh: gy: 8 (over z, core), gx: 16 (over x, y).
Axes of the slice: x: 4, y: 4, z: 4, core: 2. Of those that a mesh axis runs over, the one named last changes fastest.
Arguments:
- source_field: float32 [2, 1, 4096, 4096], P(None, None, 'gx', 'gy'), may hold values from -5 to 5
- receiver_field: float32 [2, 1, 4096, 4096], P(None, None, 'gx', 'gy'), may hold values from -5 to 5
- velocity_index: int32 [4, 4096, 4096], P(None, 'gx', 'gy'), may hold values from 0 to 63
- slowness: float32 [64], replicated, may hold values from 0.25 to 1
- freq_index: int32 [1], replicated, may hold values from 8 to 511
- root_modulus: float32 [1], replicated, may hold values from 0.9 to 1, as said below
- root_angle: float32 [1], replicated, may hold values from -3.140625 to 3.140625
Outputs:
- image: float32 [4, 4096, 4096], P(None, 'gx', 'gy')
- source_bottom: float32 [2, 1, 4096, 4096], P(None, None, 'gx', 'gy')
- receiver_top: float32 [2, 1, 4096, 4096], P(None, None, 'gx', 'gy')
The draws below stay inside these ranges and needn't reach their ends.
Inputs may be any that keep to these rules, and one draw needn't show every extreme that they name: `root_modulus`: each modulus lies strictly below 1.
All inputs are finite; a program needn't handle non-finite values.
Results may differ from the reference program's by a relative error of at most 0.0003.
Values sent between devices are 32-bit elements; how exact they have to be, the bound alone decides.
A program may use at most 128 MiB of HBM per device.

```python
import math
import jax
import jax.numpy as jnp
from jax import lax

NX = 4096
NY = 4096
FREQS = 1
DEPTH = 4
NVEL = 64


def draw_wave(key):
    shape = (2, FREQS, NX, NY)
    return jnp.clip(jax.random.normal(key, shape, jnp.float32), -5.0, 5.0)


def draw_source_field(key, part):
    return draw_wave(jax.random.fold_in(key, 11))


def draw_receiver_field(key, part):
    return draw_wave(jax.random.fold_in(key, 23))


def draw_root_modulus(key, part):
    unit = jax.random.uniform(jax.random.fold_in(key, 37), (FREQS,), jnp.float32)
    low_end = math.log(16.0)
    high_end = math.log(4096.0)
    reach = jnp.exp(low_end + (high_end - low_end) * unit)
    return jnp.exp(-1.0 / reach)


def touch_ends(entries, rng, low, largest):
    longest = entries.shape.index(max(entries.shape))
    spots = []
    for shift in (0, 1):
        where = [jax.random.randint(jax.random.fold_in(rng, axis), (), 0, length) for axis, length in enumerate(entries.shape)]
        where[longest] = (where[longest] + shift) % entries.shape[longest]
        spots.append(tuple(where))
    return entries.at[spots[0]].set(low).at[spots[1]].set(largest)


def setup_inputs(seed: int = 0) -> dict:
    splits = jax.random.split(jax.random.key(seed), 8)
    return {
        "source_field": draw_source_field(jax.random.fold_in(splits[7], 71), 0),
        "receiver_field": draw_receiver_field(jax.random.fold_in(splits[7], 71), 0),
        "velocity_index": touch_ends(jax.random.randint(splits[2], (DEPTH, NX, NY), 0, NVEL), jax.random.fold_in(splits[2], 1), 0, NVEL - 1).astype(jnp.int32),
        "slowness": jnp.clip(jnp.exp(jax.random.uniform(splits[3], (NVEL,), jnp.float32, math.log(0.25), math.log(1.0))), 0.25, 1.0),
        "freq_index": jax.random.randint(splits[4], (FREQS,), 8, 512).astype(jnp.int32),
        "root_modulus": draw_root_modulus(jax.random.fold_in(splits[7], 71), 0),
        "root_angle": jnp.clip(jax.random.uniform(splits[6], (FREQS,), jnp.float32, -3.140625, 3.140625), -3.140625, 3.140625),
    }


PHASE_UNIT = 0.05


def line_recur(wave_re, wave_im, modulus, angle, line_dim, backward):
    root_re = (modulus * jnp.cos(angle))[:, None]
    root_im = (modulus * jnp.sin(angle))[:, None]
    moved_re = jnp.moveaxis(wave_re, line_dim, 0)
    moved_im = jnp.moveaxis(wave_im, line_dim, 0)
    zeros_row = jnp.zeros_like(moved_re[0])

    def advance(carry_set, inputs):
        prev_re, prev_im, last_re, last_im = carry_set
        cur_re, cur_im = inputs
        next_re = root_re * prev_re - root_im * prev_im + last_re - (root_re * cur_re + root_im * cur_im)
        next_im = root_re * prev_im + root_im * prev_re + last_im - (root_re * cur_im - root_im * cur_re)
        return (next_re, next_im, cur_re, cur_im), (next_re, next_im)

    start_set = (zeros_row, zeros_row, zeros_row, zeros_row)
    final_set, outputs = lax.scan(advance, start_set, (moved_re, moved_im), reverse=backward)
    return jnp.moveaxis(outputs[0], 0, line_dim), jnp.moveaxis(outputs[1], 0, line_dim)


def sweep_line(wave_re, wave_im, modulus, angle, line_dim):
    ahead_re, ahead_im = line_recur(wave_re, wave_im, modulus, angle, line_dim, False)
    return line_recur(ahead_re, ahead_im, modulus, angle, line_dim, True)


def reference(source_field, receiver_field, velocity_index, slowness, freq_index, root_modulus, root_angle):
    phase_rate = freq_index.astype(jnp.float32)[:, None, None] * PHASE_UNIT
    back_angle = -root_angle

    def rotation(level_index):
        slow_cell = slowness[velocity_index[level_index]]
        phase_arg = phase_rate * slow_cell[None]
        return jnp.cos(phase_arg), jnp.sin(phase_arg)

    src_re = source_field[0]
    src_im = source_field[1]
    source_levels = []
    for level_index in range(DEPTH):
        source_levels.append((src_re, src_im))
        src_re, src_im = sweep_line(src_re, src_im, root_modulus, root_angle, 1)
        src_re, src_im = sweep_line(src_re, src_im, root_modulus, root_angle, 2)
        cos_part, sin_part = rotation(level_index)
        src_re, src_im = src_re * cos_part - src_im * sin_part, src_re * sin_part + src_im * cos_part
    rec_re = receiver_field[0]
    rec_im = receiver_field[1]
    images = [None] * DEPTH
    for level_index in reversed(range(DEPTH)):
        cos_part, sin_part = rotation(level_index)
        rec_re, rec_im = rec_re * cos_part + rec_im * sin_part, rec_im * cos_part - rec_re * sin_part
        rec_re, rec_im = sweep_line(rec_re, rec_im, root_modulus, back_angle, 2)
        rec_re, rec_im = sweep_line(rec_re, rec_im, root_modulus, back_angle, 1)
        level_re, level_im = source_levels[level_index]
        images[level_index] = jnp.sum(level_re * rec_re + level_im * rec_im, axis=0)
    return jnp.stack(images), jnp.stack([src_re, src_im]), jnp.stack([rec_re, rec_im])
```

```python
import functools

import jax
import jax.numpy as jnp
from jax import lax
from jax.experimental import pallas as pl
from jax.experimental.pallas import tpu as pltpu
from jax.sharding import PartitionSpec as P

MESH = pl.DeviceIdType.MESH
F32 = jnp.float32
BF16 = jnp.bfloat16
L = 256
DEPTH = 4
PHASE_UNIT = 0.05
ROWS = 32


def cmul(a, b):
    return a[0] * b[0] - a[1] * b[1], a[0] * b[1] + a[1] * b[0]


def split(x):
    hi = x.astype(BF16)
    lo = (x - hi.astype(F32)).astype(BF16)
    return hi, lo


def mm(a, b):
    return jnp.dot(a, b, preferred_element_type=F32)


def mm_nt(a, b):
    return lax.dot_general(a, b, (((1,), (1,)), ((), ())), preferred_element_type=F32)


def iota(shape, dim):
    return lax.broadcasted_iota(jnp.int32, shape, dim)


def build_tables(nx, ny, a, b, modulus, angle, va_ref, vb_ref, vl_ref, qx_ref, qy_ref):
    one = jnp.full((8, 128), 1.0, F32)
    m = one * modulus
    th = one * angle
    d = 1.0 - m
    z = d / (2.0 - d)
    z2 = z * z
    logm = -2.0 * z * (1.0 + z2 * (1.0 / 3.0 + z2 * (0.2 + z2 * (1.0 / 7.0 + z2 * (1.0 / 9.0)))))
    ct, st = jnp.cos(th), jnp.sin(th)
    p = (m * ct, m * st)
    kappa = d * (1.0 + m)
    den = (kappa + 2.0 * m * m * st * st, -2.0 * m * m * st * ct)
    inv = 1.0 / (den[0] * den[0] + den[1] * den[1])
    rden = (den[0] * inv, -den[1] * inv)
    gamma = (kappa * kappa * rden[0], kappa * kappa * rden[1])
    beta = (-gamma[0], -gamma[1])
    alpha = cmul((2.0 * kappa * st * st, 2.0 * kappa * st * ct), rden)
    alpha_p = cmul(alpha, p)
    diag = (p[0] * p[0] - p[1] * p[1] + gamma[0], -2.0 * p[0] * p[1] + gamma[1])

    def sc(v):
        return v[0][0:1, 0:1], v[1][0:1, 0:1]

    row = iota((8, L), 0)
    col = iota((8, L), 1)
    expo = jnp.where(row == 0, col, jnp.where(row == 1, L - 1 - col, -col)).astype(F32)
    mag = jnp.exp(expo * logm[0:1, 0:1])
    turn = expo * th[0:1, 0:1]
    pw = (mag * jnp.cos(turn), mag * jnp.sin(turn))
    pw_t = tuple(jnp.concatenate([v] * 16, axis=0).T for v in pw)

    def prow(i):
        return pw[0][i : i + 1, :], pw[1][i : i + 1, :]

    def pcol(i):
        return pw_t[0][:, i : i + 1], pw_t[1][:, i : i + 1]

    h_r, g_r, n_r = prow(0), prow(1), prow(2)
    h_c, g_c, n_c = pcol(0), pcol(1), pcol(2)

    ii = iota((L, L), 0)
    jj = iota((L, L), 1)
    low = ii >= jj
    left = tuple(jnp.where(low, h_c[t], n_c[t]) for t in (0, 1))
    right = tuple(jnp.where(low, n_r[t], h_r[t]) for t in (0, 1))
    k_full = cmul(sc(alpha), cmul(left, right))
    dg = sc(diag)
    k_re = jnp.where(ii == jj, dg[0], k_full[0])
    k_im = jnp.where(ii == jj, dg[1], k_full[1])
    for part, sign_ab in ((k_re, None), (k_im, 1)):
        hi, lo = split(part)
        for which, piece in ((0, hi), (1, lo)):
            if sign_ab is None:
                spots_a = (((0, 0), piece), ((L, L), piece))
                spots_b = spots_a
            else:
                spots_a = (((0, L), -piece), ((L, 0), piece))
                spots_b = (((0, L), piece), ((L, 0), -piece))
            for (r0, c0), val in spots_a:
                if which == 0:
                    va_ref[r0 : r0 + L, c0 : c0 + L] = val
                    va_ref[r0 : r0 + L, 2 * L + c0 : 3 * L + c0] = val
                else:
                    va_ref[r0 : r0 + L, 4 * L + c0 : 5 * L + c0] = val
            for (r0, c0), val in spots_b:
                if which == 0:
                    vb_ref[r0 : r0 + L, c0 : c0 + L] = val
                    vb_ref[2 * L + r0 : 3 * L + r0, c0 : c0 + L] = val
                else:
                    vb_ref[4 * L + r0 : 5 * L + r0, c0 : c0 + L] = val

    r8 = iota((8, L), 0)
    q8 = r8 & 3
    v_re = jnp.where(q8 == 0, g_r[0], jnp.where(q8 == 1, g_r[1], jnp.where(q8 == 2, h_r[0], h_r[1])))
    v_im = jnp.where(q8 == 0, -g_r[1], jnp.where(q8 == 1, g_r[0], jnp.where(q8 == 2, -h_r[1], h_r[0])))
    for h in (0, 1):
        mine = (r8 >> 2) == h
        for part, val in ((0, v_re), (1, v_im)):
            val = jnp.where(mine, val, 0.0)
            hi = val.astype(BF16).astype(F32)
            lo = val - hi
            vl_ref[h, :, part * L : (part + 1) * L] = jnp.concatenate([hi, lo], axis=0).astype(BF16)
            vl_ref[h, :, (2 + part) * L : (3 + part) * L] = jnp.concatenate([hi, jnp.zeros_like(hi)], axis=0).astype(BF16)

    rr = iota((8, 128), 0)
    kk = iota((8, 128), 1)
    is_x = rr < 2
    target = jnp.where(is_x, a, 2 * b + (rr >> 1) - 1)
    source = jnp.where(is_x, kk >> 3, kk >> 2)
    count = jnp.where(is_x, nx, 2 * ny)
    is_s = (rr & 1) == 0
    is_e = (kk & 3) >= 2
    is_i = (kk & 1) == 1
    steps = jnp.where(is_s, target - 1 - source, jnp.where(is_e, source - target - 1, 2 * count - 2 - target - source))
    valid = (steps >= 0) & jnp.logical_not(is_s & is_e)
    use_beta = jnp.logical_not(is_s) & jnp.logical_not(is_e)
    n = jnp.maximum(steps, 0).astype(F32)
    th_l = th * float(L)
    wraps = jnp.floor(th_l * 0.15915494309189535 + 0.5)
    th_l = (th_l - wraps * 6.28125) - wraps * 0.0019353071795864769
    mag = jnp.exp(n * (logm * float(L)))
    om = (mag * jnp.cos(n * th_l), mag * jnp.sin(n * th_l))
    coef = (jnp.where(use_beta, beta[0], alpha_p[0]), jnp.where(use_beta, beta[1], alpha_p[1]))
    om = cmul(om, coef)
    om = (jnp.where(is_i, -om[1], om[0]), jnp.where(is_i, om[0], om[1]))
    om = tuple(jnp.where(valid, v, 0.0) for v in om)
    om_t = tuple(jnp.concatenate([v] * 16, axis=0).T for v in om)

    rx, ry = 8 * nx, 8 * ny
    half = (iota((1, 128), 1) >> 2) & 1
    for h in (0, 1):
        keep = half == h
        w_s = tuple(jnp.where(keep, om[t][0:1, :], 0.0)[:, :rx] for t in (0, 1))
        w_t = tuple(jnp.where(keep, om[t][1:2, :], 0.0)[:, :rx] for t in (0, 1))
        q1 = cmul(h_c, w_s)
        q2 = cmul(g_c, w_t)
        for part in (0, 1):
            hi, lo = split(q1[part] + q2[part])
            r0 = (2 * h + part) * L
            qx_ref[r0 : r0 + L, 0:rx] = hi
            qx_ref[r0 : r0 + L, rx : 2 * rx] = hi
            qx_ref[r0 : r0 + L, 2 * rx : 3 * rx] = lo
        w_s = tuple(om_t[t][:ry, 2 + 2 * h : 3 + 2 * h] for t in (0, 1))
        w_t = tuple(om_t[t][:ry, 3 + 2 * h : 4 + 2 * h] for t in (0, 1))
        q1 = cmul(w_s, h_r)
        q2 = cmul(w_t, g_r)
        for part in (0, 1):
            hi, lo = split(q1[part] + q2[part])
            c0 = (2 * h + part) * L
            qy_ref[0:ry, c0 : c0 + L] = hi
            qy_ref[ry : 2 * ry, c0 : c0 + L] = hi
            qy_ref[2 * ry : 3 * ry, c0 : c0 + L] = lo
    if 3 * ry < L:
        qy_ref[3 * ry : L, :] = jnp.zeros((L - 3 * ry, 4 * L), BF16)


def kernel(
    nx, ny, wide,
    src, rec, vidx, slow, freq, mod, ang,
    img_o, bot_o, top_o,
    slev, rlev, rin, vin, cosb, sinb, tab, u_ref, hl, hly, xo, yo, imgb,
    va, vb, vl, qx, qy, gxb, gyb,
    in_sem, out_sem, send_sem, recv_sem,
):
    a = lax.axis_index("gx")
    b = lax.axis_index("gy")
    ins = [
        pltpu.make_async_copy(src, slev.at[0], in_sem.at[0]),
        pltpu.make_async_copy(rec, rin, in_sem.at[1]),
        pltpu.make_async_copy(vidx, vin, in_sem.at[2]),
    ]
    for copy in ins:
        copy.start()

    if nx == 16 and wide:
        ax, ay = a // 4, a % 4
        far = sorted(((i, j) for i in range(4) for j in range(4) if i or j), key=lambda t: -(min(t[0], 4 - t[0]) + min(t[1], 4 - t[1])))
        x_peers = [lax.rem(ax + i, 4) * 4 + lax.rem(ay + j, 4) for i, j in far]
    else:
        x_peers = [lax.rem(a + o, nx) for o in range(1, nx)]
    order = sorted(range(1, ny), key=lambda o: -min(o // 2, (ny - o) // 2))
    y_peers = [lax.rem(b + o, ny) for o in order]

    barrier = pltpu.get_barrier_semaphore()
    for peer in x_peers:
        pl.semaphore_signal(barrier, inc=1, device_id={"gx": peer}, device_id_type=MESH)
    for peer in y_peers:
        pl.semaphore_signal(barrier, inc=1, device_id={"gy": peer}, device_id_type=MESH)

    build_tables(nx, ny, a, b, mod[0], ang[0], va, vb, vl, qx, qy)
    tab[...] = jnp.zeros((8, 128), F32)
    tab[0:1, 0:64] = slow[...]
    rate = jnp.full((8, 128), 1.0, F32) * freq[0].astype(F32) * PHASE_UNIT
    arg = rate * tab[...]
    cos_tab = jnp.broadcast_to(jnp.cos(arg)[0:1, :], (ROWS, 128))
    sin_tab = jnp.broadcast_to(jnp.sin(arg)[0:1, :], (ROWS, 128))

    def rows_loop(body):
        def go(i, carry):
            body(pl.multiple_of(i * ROWS, ROWS))
            return carry

        lax.fori_loop(0, L // ROWS, go, 0)

    def look_up(level):
        def body(r):
            for c in range(4):
                idx = vin[level, pl.ds(r, ROWS), c * 128 : (c + 1) * 128]
                cosb[level, pl.ds(r, ROWS), c * 128 : (c + 1) * 128] = jnp.take_along_axis(cos_tab, idx, axis=1, mode="promise_in_bounds")
                sinb[level, pl.ds(r, ROWS), c * 128 : (c + 1) * 128] = jnp.take_along_axis(sin_tab, idx, axis=1, mode="promise_in_bounds")

        rows_loop(body)

    def put_x(r, h, re, im):
        cols = slice(h * L, (h + 1) * L)
        for part, val in ((0, re), (1, im)):
            hi, lo = split(val)
            hl[pl.ds(part * L + r, ROWS), cols] = hi
            hl[pl.ds((2 + part) * L + r, ROWS), cols] = lo

    def x_copies(f, k):
        slot = gxb.at[f, k, a]
        return [
            pltpu.make_async_remote_copy(slot, slot, send_sem.at[0, f, k], recv_sem.at[0, f, k], device_id={"gx": peer}, device_id_type=MESH)
            for peer in x_peers
        ]

    def y_copies(f, k):
        slot = gyb.at[f, k, b]
        return [
            pltpu.make_async_remote_copy(slot, slot, send_sem.at[1, f, k], recv_sem.at[1, f, k], device_id={"gy": peer}, device_id_type=MESH)
            for peer in y_peers
        ]

    def all_x(f, k):
        block = gxb.at[f, k, pl.ds(0, nx - 1)]
        return pltpu.make_async_remote_copy(block, block, send_sem.at[0, f, k], recv_sem.at[0, f, k], device_id={"gx": a}, device_id_type=MESH)

    def all_y(f, k):
        block = gyb.at[f, k, pl.ds(0, ny - 1)]
        return pltpu.make_async_remote_copy(block, block, send_sem.at[1, f, k], recv_sem.at[1, f, k], device_id={"gy": b}, device_id_type=MESH)

    def x_carry(f, k):
        acc = None
        for h in (0, 1):
            part = mm(vl[h], hl[:, h * L : (h + 1) * L])
            acc = part if acc is None else acc + part
        gxb[f, k, a] = acc[0:8] + acc[8:16]

    def x_local(f):
        u_ref[f] = mm(va[:, 0 : 4 * L], hl[...]) + mm(va[:, 4 * L : 6 * L], hl[0 : 2 * L, :])

    def x_start(f, k):
        x_carry(f, k)
        for copy in x_copies(f, k):
            copy.start()
        x_local(f)

    def x_end(f, k):
        all_x(f, k).wait_recv()
        rx = 8 * nx
        hi, lo = split(gxb[f, k].reshape(rx, L))
        g3 = jnp.concatenate([hi, lo, hi], axis=0)
        xo[...] = mm(qx[...], g3)

        def body(r):
            for h in (0, 1):
                for part in (0, 1):
                    val = u_ref[f, pl.ds(part * L + r, ROWS), h * L : (h + 1) * L] + xo[pl.ds((2 * h + part) * L + r, ROWS), :]
                    hi, lo = split(val)
                    hly[h, pl.ds(r, ROWS), part * L : (part + 1) * L] = hi
                    hly[h, pl.ds(r, ROWS), (2 + part) * L : (3 + part) * L] = lo

        rows_loop(body)

    def y_start(f, k):
        acc = None
        for h in (0, 1):
            part = mm_nt(vl[h], hly[h])
            acc = part if acc is None else acc + part
        gyb[f, k, b] = acc[0:8] + acc[8:16]
        for copy in y_copies(f, k):
            copy.start()
        for h in (0, 1):
            out = mm(hly[h], vb[0 : 4 * L, :]) + mm(hly[h, :, 0 : 2 * L], vb[4 * L : 6 * L, :])
            u_ref[f, 0:L, h * L : (h + 1) * L] = out[:, 0:L]
            u_ref[f, L : 2 * L, h * L : (h + 1) * L] = out[:, L : 2 * L]

    def y_end(f, k):
        all_y(f, k).wait_recv()
        ry = 8 * ny
        g = gyb[f, k].reshape(ry, L)
        hi = g.astype(BF16).astype(F32)
        lo = g - hi
        pieces = [hi, lo, hi]
        if 3 * ry < L:
            pieces.append(jnp.zeros((L - 3 * ry, L), F32))
        yo[...] = mm(jnp.concatenate(pieces, axis=0).T.astype(BF16), qy[...])

    def y_value(f, r, h):
        cols = slice(h * L, (h + 1) * L)
        re = u_ref[f, pl.ds(r, ROWS), cols] + yo[pl.ds(r, ROWS), 2 * h * L : (2 * h + 1) * L]
        im = u_ref[f, pl.ds(L + r, ROWS), cols] + yo[pl.ds(r, ROWS), (2 * h + 1) * L : (2 * h + 2) * L]
        return re, im

    def turn(level, r, h, re, im):
        cols = slice(h * L, (h + 1) * L)
        c = cosb[level, pl.ds(r, ROWS), cols]
        s = sinb[level, pl.ds(r, ROWS), cols]
        return re * c - im * s, re * s + im * c

    def source_turn(k):
        def body(r):
            for h in (0, 1):
                cols = slice(h * L, (h + 1) * L)
                re, im = turn(k, r, h, *y_value(0, r, h))
                slev[k + 1, pl.ds(r, ROWS), cols] = re
                slev[k + 1, pl.ds(L + r, ROWS), cols] = im
                put_x(r, h, re, im)

        rows_loop(body)

    def receiver_turn(k):
        level = jnp.maximum(DEPTH - 2 - k, 0)

        def body(r):
            for h in (0, 1):
                cols = slice(h * L, (h + 1) * L)
                re, im = y_value(1, r, h)
                rlev[DEPTH - 1 - k, pl.ds(r, ROWS), cols] = re
                rlev[DEPTH - 1 - k, pl.ds(L + r, ROWS), cols] = im
                put_x(r, h, *turn(level, r, h, re, im))

        rows_loop(body)

    def image_copy(z):
        return pltpu.make_async_copy(imgb.at[z], img_o.at[z], out_sem.at[z])

    def image(z):
        def body(r):
            imgb[z, pl.ds(r, ROWS), :] = (
                slev[z, pl.ds(r, ROWS), :] * rlev[z, pl.ds(r, ROWS), :]
                - slev[z, pl.ds(L + r, ROWS), :] * rlev[z, pl.ds(L + r, ROWS), :]
            )

        rows_loop(body)
        image_copy(z).start()

    ins[0].wait()

    def first_source(r):
        for h in (0, 1):
            cols = slice(h * L, (h + 1) * L)
            put_x(r, h, slev[0, pl.ds(r, ROWS), cols], slev[0, pl.ds(L + r, ROWS), cols])

    rows_loop(first_source)
    pl.semaphore_wait(barrier, (nx - 1) + (ny - 1))
    x_start(0, 0)
    ins[1].wait()
    ins[2].wait()
    look_up(DEPTH - 1)

    def first_receiver(r):
        for h in (0, 1):
            cols = slice(h * L, (h + 1) * L)
            put_x(r, h, *turn(DEPTH - 1, r, h, rin[pl.ds(r, ROWS), cols], -rin[pl.ds(L + r, ROWS), cols]))

    rows_loop(first_receiver)
    x_start(1, 0)
    for level in range(DEPTH - 1):
        look_up(level)

    def step(k, carry):
        for f in (0, 1):
            x_end(f, k)
            y_start(f, k)
        y_end(0, k)
        source_turn(k)

        @pl.when(k < DEPTH - 1)
        def _():
            x_start(0, k + 1)

        y_end(1, k)
        receiver_turn(k)

        @pl.when(k < DEPTH - 1)
        def _():
            x_start(1, k + 1)

        @pl.when(k == 1)
        def _():
            image(2)

        @pl.when(k == 2)
        def _():
            image(3)
            image(1)

        return carry

    lax.fori_loop(0, DEPTH, step, 0)

    bottom = pltpu.make_async_copy(slev.at[DEPTH], bot_o, out_sem.at[DEPTH])
    bottom.start()

    def flip(r):
        rin[pl.ds(r, ROWS), :] = rlev[0, pl.ds(r, ROWS), :]
        rin[pl.ds(L + r, ROWS), :] = -rlev[0, pl.ds(L + r, ROWS), :]

    rows_loop(flip)
    top = pltpu.make_async_copy(rin, top_o, out_sem.at[DEPTH + 1])
    top.start()
    image(0)
    for f in (0, 1):
        for k in range(DEPTH):
            all_x(f, k).wait_send()
            all_y(f, k).wait_send()
    for z in range(DEPTH):
        image_copy(z).wait()
    bottom.wait()
    top.wait()


def solution(mesh):
    nx, ny = mesh.shape["gx"], mesh.shape["gy"]
    rx = 8 * nx

    def on_device(source_field, receiver_field, velocity_index, slowness, freq_index, root_modulus, root_angle):
        width = source_field.shape[3]
        any_spec = pl.BlockSpec(memory_space=pl.ANY)
        smem = pl.BlockSpec(memory_space=pltpu.SMEM)
        vmem = pl.BlockSpec(memory_space=pltpu.VMEM)
        image, bottom, top = pl.pallas_call(
            functools.partial(kernel, nx, ny, True),
            out_shape=(
                jax.ShapeDtypeStruct((DEPTH, L, width), F32),
                jax.ShapeDtypeStruct((2 * L, width), F32),
                jax.ShapeDtypeStruct((2 * L, width), F32),
            ),
            in_specs=[any_spec, any_spec, any_spec, vmem, smem, smem, smem],
            out_specs=(any_spec, any_spec, any_spec),
            scratch_shapes=[
                pltpu.VMEM((DEPTH + 1, 2 * L, width), F32),
                pltpu.VMEM((DEPTH, 2 * L, width), F32),
                pltpu.VMEM((2 * L, width), F32),
                pltpu.VMEM((DEPTH, L, width), jnp.int32),
                pltpu.VMEM((DEPTH, L, width), F32),
                pltpu.VMEM((DEPTH, L, width), F32),
                pltpu.VMEM((8, 128), F32),
                pltpu.VMEM((2, 2 * L, width), F32),
                pltpu.VMEM((4 * L, width), BF16),
                pltpu.VMEM((2, L, 4 * L), BF16),
                pltpu.VMEM((4 * L, L), F32),
                pltpu.VMEM((L, 4 * L), F32),
                pltpu.VMEM((DEPTH, L, width), F32),
                pltpu.VMEM((2 * L, 6 * L), BF16),
                pltpu.VMEM((6 * L, 2 * L), BF16),
                pltpu.VMEM((2, 16, 4 * L), BF16),
                pltpu.VMEM((4 * L, 3 * rx), BF16),
                pltpu.VMEM((L, 4 * L), BF16),
                pltpu.VMEM((2, DEPTH, nx, 8, L), F32),
                pltpu.VMEM((2, DEPTH, ny, 8, L), F32),
                pltpu.SemaphoreType.DMA((3,)),
                pltpu.SemaphoreType.DMA((DEPTH + 2,)),
                pltpu.SemaphoreType.DMA((2, 2, DEPTH)),
                pltpu.SemaphoreType.DMA((2, 2, DEPTH)),
            ],
            compiler_params=pltpu.CompilerParams(collective_id=0, has_side_effects=True, vmem_limit_bytes=56 * 2**20),
        )(
            source_field.reshape(2 * L, width),
            receiver_field.reshape(2 * L, width),
            velocity_index,
            slowness.reshape(1, -1),
            freq_index,
            root_modulus,
            root_angle,
        )
        return image, bottom.reshape(source_field.shape), top.reshape(receiver_field.shape)

    wave = P(None, None, "gx", "gy")
    return jax.shard_map(
        on_device,
        mesh=mesh,
        in_specs=(wave, wave, P(None, "gx", "gy"), P(), P(), P(), P()),
        out_specs=(P(None, "gx", "gy"), wave, wave),
        check_vma=False,
    )
```

```python
import functools

import jax
import jax.numpy as jnp
from jax import lax
from jax.experimental import pallas as pl
from jax.experimental.pallas import tpu as pltpu
from jax.sharding import PartitionSpec as P

MESH = pl.DeviceIdType.MESH
F32 = jnp.float32
BF16 = jnp.bfloat16
L = 256
DEPTH = 4
PHASE_UNIT = 0.05
ROWS = 32


def cmul(a, b):
    return a[0] * b[0] - a[1] * b[1], a[0] * b[1] + a[1] * b[0]


def split(x):
    hi = x.astype(BF16)
    lo = (x - hi.astype(F32)).astype(BF16)
    return hi, lo


def mm(a, b):
    return jnp.dot(a, b, preferred_element_type=F32)


def mm_nt(a, b):
    return lax.dot_general(a, b, (((1,), (1,)), ((), ())), preferred_element_type=F32)


def iota(shape, dim):
    return lax.broadcasted_iota(jnp.int32, shape, dim)


def build_tables(nx, ny, a, b, modulus, angle, va_ref, vb_ref, vl_ref, kw_ref, qx_ref, qy_ref, qc_ref):
    one = jnp.full((8, 128), 1.0, F32)
    m = one * modulus
    th = one * angle
    d = 1.0 - m
    z = d / (2.0 - d)
    z2 = z * z
    logm = -2.0 * z * (1.0 + z2 * (1.0 / 3.0 + z2 * (0.2 + z2 * (1.0 / 7.0 + z2 * (1.0 / 9.0)))))
    ct, st = jnp.cos(th), jnp.sin(th)
    p = (m * ct, m * st)
    kappa = d * (1.0 + m)
    den = (kappa + 2.0 * m * m * st * st, -2.0 * m * m * st * ct)
    inv = 1.0 / (den[0] * den[0] + den[1] * den[1])
    rden = (den[0] * inv, -den[1] * inv)
    gamma = (kappa * kappa * rden[0], kappa * kappa * rden[1])
    beta = (-gamma[0], -gamma[1])
    alpha = cmul((2.0 * kappa * st * st, 2.0 * kappa * st * ct), rden)
    alpha_p = cmul(alpha, p)
    diag = (p[0] * p[0] - p[1] * p[1] + gamma[0], -2.0 * p[0] * p[1] + gamma[1])

    def sc(v):
        return v[0][0:1, 0:1], v[1][0:1, 0:1]

    row = iota((8, L), 0)
    col = iota((8, L), 1)
    expo = jnp.where(row == 0, col, jnp.where(row == 1, L - 1 - col, -col)).astype(F32)
    mag = jnp.exp(expo * logm[0:1, 0:1])
    turn = expo * th[0:1, 0:1]
    pw = (mag * jnp.cos(turn), mag * jnp.sin(turn))
    pw_t = tuple(jnp.concatenate([v] * 16, axis=0).T for v in pw)

    def prow(i):
        return pw[0][i : i + 1, :], pw[1][i : i + 1, :]

    def pcol(i):
        return pw_t[0][:, i : i + 1], pw_t[1][:, i : i + 1]

    h_r, g_r, n_r = prow(0), prow(1), prow(2)
    h_c, g_c, n_c = pcol(0), pcol(1), pcol(2)

    ii = iota((L, L), 0)
    jj = iota((L, L), 1)
    low = ii >= jj
    left = tuple(jnp.where(low, h_c[t], n_c[t]) for t in (0, 1))
    right = tuple(jnp.where(low, n_r[t], h_r[t]) for t in (0, 1))
    k_full = cmul(sc(alpha), cmul(left, right))
    dg = sc(diag)
    k_re = jnp.where(ii == jj, dg[0], k_full[0])
    k_im = jnp.where(ii == jj, dg[1], k_full[1])
    for part, sign_ab in ((k_re, None), (k_im, 1)):
        hi, lo = split(part)
        for which, piece in ((0, hi), (1, lo)):
            if sign_ab is None:
                spots_a = (((0, 0), piece), ((L, L), piece))
                spots_b = spots_a
            else:
                spots_a = (((0, L), -piece), ((L, 0), piece))
                spots_b = (((0, L), piece), ((L, 0), -piece))
            for (r0, c0), val in spots_a:
                if which == 0:
                    va_ref[r0 : r0 + L, c0 : c0 + L] = val
                    va_ref[r0 : r0 + L, 2 * L + c0 : 3 * L + c0] = val
                else:
                    va_ref[r0 : r0 + L, 4 * L + c0 : 5 * L + c0] = val
            for (r0, c0), val in spots_b:
                if which == 0:
                    vb_ref[r0 : r0 + L, c0 : c0 + L] = val
                    vb_ref[2 * L + r0 : 3 * L + r0, c0 : c0 + L] = val
                else:
                    vb_ref[4 * L + r0 : 5 * L + r0, c0 : c0 + L] = val

    r8 = iota((8, L), 0)
    end8 = (r8 & 1) == 1
    v_re = jnp.where(end8, h_r[0], g_r[0])
    v_im = jnp.where(end8, h_r[1], g_r[1])
    imag8 = r8 >= 4
    v_parts = (jnp.where(imag8, v_im, v_re), jnp.where(imag8, v_re, -v_im))
    for h in (0, 1):
        mine = ((r8 >> 1) & 1) == h
        for part in (0, 1):
            val = jnp.where(mine, v_parts[part], 0.0)
            hi = val.astype(BF16).astype(F32)
            lo = val - hi
            vl_ref[h, :, part * L : (part + 1) * L] = jnp.concatenate([hi, lo], axis=0).astype(BF16)
            vl_ref[h, :, (2 + part) * L : (3 + part) * L] = jnp.concatenate([hi, jnp.zeros_like(hi)], axis=0).astype(BF16)

    lane = iota((L, 128), 1)
    end_l = ((lane >> 1) & 1) == 1
    imag_l = (lane & 1) == 1
    c_re = jnp.where(end_l, h_c[0], g_c[0])
    c_im = jnp.where(end_l, h_c[1], g_c[1])
    for c0, val in (
        (0, k_re), (L, k_im),
        (2 * L, jnp.where(imag_l, c_im, c_re)),
        (2 * L + 128, jnp.where(imag_l, c_re, -c_im)),
    ):
        hi, lo = split(val)
        kw_ref[0, :, c0 : c0 + val.shape[1]] = hi
        kw_ref[1, :, c0 : c0 + val.shape[1]] = lo

    rr = iota((16, 128), 0)
    kk = iota((16, 128), 1)
    is_x = rr < 2
    is_c = rr >= 6
    target = jnp.where(is_x, a, 2 * b + jnp.where(is_c, (rr - 6) >> 1, (rr - 2) >> 1))
    source = jnp.where(is_x | is_c, kk >> 3, 2 * (kk >> 3) + ((kk >> 1) & 1))
    count = jnp.where(is_x, nx, 2 * ny)
    is_s = (rr & 1) == 0
    is_e = jnp.where(is_c, (kk >> 1) & 1, kk & 1) == 1
    is_i = jnp.where(is_c, kk & 1, (kk >> 2) & 1) == 1
    steps = jnp.where(is_s, target - 1 - source, jnp.where(is_e, source - target - 1, 2 * count - 2 - target - source))
    valid = (steps >= 0) & jnp.logical_not(is_s & is_e)
    use_beta = jnp.logical_not(is_s) & jnp.logical_not(is_e)
    n = jnp.maximum(steps, 0).astype(F32)
    th_l = th * float(L)
    wraps = jnp.floor(th_l * 0.15915494309189535 + 0.5)
    th_l = (th_l - wraps * 6.28125) - wraps * 0.0019353071795864769
    mag = jnp.exp(n * (logm[0:1, :] * float(L)))
    om = (mag * jnp.cos(n * th_l[0:1, :]), mag * jnp.sin(n * th_l[0:1, :]))
    coef = tuple(jnp.where(use_beta, beta[t][0:1, :], alpha_p[t][0:1, :]) for t in (0, 1))
    om = cmul(om, coef)
    om = (jnp.where(is_i, -om[1], om[0]), jnp.where(is_i, om[0], om[1]))
    om = tuple(jnp.where(valid, v, 0.0) for v in om)
    om_t = tuple(jnp.concatenate([v] * 8, axis=0).T for v in om)

    rx, ry = 8 * nx, 8 * ny
    half = (iota((1, 128), 1) >> 1) & 1
    for h in (0, 1):
        keep = half == h
        w_s = tuple(jnp.where(keep, om[t][0:1, :], 0.0)[:, :rx] for t in (0, 1))
        w_t = tuple(jnp.where(keep, om[t][1:2, :], 0.0)[:, :rx] for t in (0, 1))
        q1 = cmul(h_c, w_s)
        q2 = cmul(g_c, w_t)
        for part in (0, 1):
            hi, lo = split(q1[part] + q2[part])
            r0 = (2 * h + part) * L
            qx_ref[r0 : r0 + L, 0:rx] = hi
            qx_ref[r0 : r0 + L, rx : 2 * rx] = hi
            qx_ref[r0 : r0 + L, 2 * rx : 3 * rx] = lo
        for first, size, ref in ((2, ry, qy_ref), (6, 128, qc_ref)):
            w_s = tuple(om_t[t][:size, first + 2 * h : first + 2 * h + 1] for t in (0, 1))
            w_t = tuple(om_t[t][:size, first + 2 * h + 1 : first + 2 * h + 2] for t in (0, 1))
            q1 = cmul(w_s, h_r)
            q2 = cmul(w_t, g_r)
            for part in (0, 1):
                hi, lo = split(q1[part] + q2[part])
                c0 = ((2 * h + part) if first == 2 else (2 * part + h)) * L
                ref[0:size, c0 : c0 + L] = hi
                ref[size : 2 * size, c0 : c0 + L] = hi
                ref[2 * size : 3 * size, c0 : c0 + L] = lo
    if 3 * ry < L:
        qy_ref[3 * ry : L, :] = jnp.zeros((L - 3 * ry, 4 * L), BF16)


def kernel(
    nx, ny,
    src, rec, vidx, slow, freq, mod, ang,
    img_o, bot_o, top_o,
    slev, rlev, rin, vin, cosb, sinb, tab, u_ref, w_ref, hl, hly, xo, yo, imgb,
    va, vb, vl, kw, qx, qy, qc, gxb, gyb, ccb,
    in_sem, out_sem, send_sem, recv_sem,
):
    a = lax.axis_index("gx")
    b = lax.axis_index("gy")
    ins = [
        pltpu.make_async_copy(src, slev.at[0], in_sem.at[0]),
        pltpu.make_async_copy(rec, rin, in_sem.at[1]),
        pltpu.make_async_copy(vidx, vin, in_sem.at[2]),
    ]
    for copy in ins:
        copy.start()

    def ring(i):
        return min(i, 4 - i)

    if nx == 16:
        ax, ay = a // 4, a % 4
        x_peers = [(ring(i) + ring(j), lax.rem(ax + i, 4) * 4 + lax.rem(ay + j, 4)) for i in range(4) for j in range(4) if i or j]
    else:
        x_peers = [(0, lax.rem(a + o, nx)) for o in range(1, nx)]
    y_peers = [(min(o // 2, (ny - o) // 2), lax.rem(b + o, ny)) for o in range(1, ny)]
    peers = [(d, 0, {"gx": p}) for d, p in x_peers] + [(d, 1, {"gy": p}) for d, p in y_peers]
    peers += [(d, 3, {"gx": p}) for d, p in x_peers] + [(d, 4, {"gy": p}) for d, p in y_peers]
    peers += [(d + e, 2, {"gx": p, "gy": q}) for d, p in x_peers for e, q in y_peers]
    peers.sort(key=lambda t: (-t[0], t[1]))

    barrier = pltpu.get_barrier_semaphore()
    for _, kind, peer in peers:
        if kind < 3:
            pl.semaphore_signal(barrier, inc=1, device_id=peer, device_id_type=MESH)

    if ny < 8:
        ccb[...] = jnp.zeros_like(ccb)
    build_tables(nx, ny, a, b, mod[0], ang[0], va, vb, vl, kw, qx, qy, qc)
    tab[...] = jnp.zeros((8, 128), F32)
    tab[0:1, 0:64] = slow[...]
    rate = jnp.full((8, 128), 1.0, F32) * freq[0].astype(F32) * PHASE_UNIT
    arg = rate * tab[...]
    cos_tab = jnp.broadcast_to(jnp.cos(arg)[0:1, :], (ROWS, 128))
    sin_tab = jnp.broadcast_to(jnp.sin(arg)[0:1, :], (ROWS, 128))

    def rows_loop(body):
        def go(i, carry):
            body(pl.multiple_of(i * ROWS, ROWS))
            return carry

        lax.fori_loop(0, L // ROWS, go, 0)

    def look_up(level):
        def body(r):
            for c in range(4):
                idx = vin[level, pl.ds(r, ROWS), c * 128 : (c + 1) * 128]
                cosb[level, pl.ds(r, ROWS), c * 128 : (c + 1) * 128] = jnp.take_along_axis(cos_tab, idx, axis=1, mode="promise_in_bounds")
                sinb[level, pl.ds(r, ROWS), c * 128 : (c + 1) * 128] = jnp.take_along_axis(sin_tab, idx, axis=1, mode="promise_in_bounds")

        rows_loop(body)

    def put_x(r, h, re, im):
        cols = slice(h * L, (h + 1) * L)
        for part, val in ((0, re), (1, im)):
            hi, lo = split(val)
            hl[pl.ds(part * L + r, ROWS), cols] = hi
            hl[pl.ds((2 + part) * L + r, ROWS), cols] = lo

    def slot(kind, f, k):
        if kind == 0:
            return gxb.at[f, k, a]
        if kind == 1:
            return gyb.at[f, k, b]
        return ccb.at[f, k, a, pl.ds(b, 1)]

    def arrivals(kind, f, k):
        block = (
            gxb.at[f, k, pl.ds(0, nx - 1)],
            gyb.at[f, k, pl.ds(0, ny - 1)],
            ccb.at[f, k, pl.ds(0, nx - 1), pl.ds(0, ny - 1)],
            ccb.at[f, k, pl.ds(0, nx - 1), pl.ds(0, 1)],
            ccb.at[f, k, 0, pl.ds(0, ny - 1)],
        )[kind]
        return pltpu.make_async_remote_copy(block, block, send_sem.at[kind, f, k], recv_sem.at[kind, f, k], device_id={"gx": a}, device_id_type=MESH)

    row8 = iota((8, L), 0)
    swap_sign = jnp.where(row8 < 4, -1.0, 1.0).astype(F32)
    lane8 = iota((8, 128), 1)
    corner_mask = (((lane8 >> 2) & 3) == iota((8, 128), 0)) & ((lane8 >> 4) == b)

    def local(f):
        w_ref[...] = mm(va[:, 0 : 4 * L], hl[...]) + mm(va[:, 4 * L : 6 * L], hl[0 : 2 * L, :])

        def body(r):
            for h in (0, 1):
                for part in (0, 1):
                    hi, lo = split(w_ref[pl.ds(part * L + r, ROWS), h * L : (h + 1) * L])
                    hly[h, pl.ds(r, ROWS), part * L : (part + 1) * L] = hi
                    hly[h, pl.ds(r, ROWS), (2 + part) * L : (3 + part) * L] = lo

        rows_loop(body)
        for h in (0, 1):
            out = mm(hly[h], vb[0 : 4 * L, :]) + mm(hly[h, :, 0 : 2 * L], vb[4 * L : 6 * L, :])
            u_ref[f, 0:L, h * L : (h + 1) * L] = out[:, 0:L]
            u_ref[f, L : 2 * L, h * L : (h + 1) * L] = out[:, L : 2 * L]

    def start(f, k):
        acc_x = acc_y = jnp.zeros((16, L), F32)
        for h in (0, 1):
            cols = slice(h * L, (h + 1) * L)
            acc_x = acc_x + mm(vl[h], hl[:, cols])
            for i in range(4):
                acc_y = acc_y + mm_nt(vl[h, :, i * L : (i + 1) * L], hl[i * L : (i + 1) * L, cols])
        carries = jnp.concatenate([acc_x[0:8] + acc_x[8:16], acc_y[0:8] + acc_y[8:16]], axis=0)
        hi = carries.astype(BF16).astype(F32)
        both = jnp.concatenate([hi, carries - hi], axis=0).astype(BF16)
        out = mm(both, kw[0])
        out = out[0:16] + out[16:32] + mm(both[0:16], kw[1])
        gxb[f, k, a] = out[0:8, 0:L] + swap_sign * pltpu.roll(out[0:8, L : 2 * L], 4, 0)
        gyb[f, k, b] = out[8:16, 0:L] + swap_sign * pltpu.roll(out[8:16, L : 2 * L], 4, 0)
        corner = out[0:8, 2 * L : 2 * L + 128] + pltpu.roll(out[0:8, 2 * L + 128 : 3 * L], 4, 0)
        ccb[f, k, a, pl.ds(b, 1)] = jnp.sum(jnp.where(corner_mask, corner, 0.0), axis=0, keepdims=True)
        for _, kind, peer in peers:
            here = slot(kind, f, k)
            pltpu.make_async_remote_copy(here, here, send_sem.at[kind, f, k], recv_sem.at[kind, f, k], device_id=peer, device_id_type=MESH).start()
        local(f)

    def finish(f, k):
        for kind in range(5):
            arrivals(kind, f, k).wait_recv()
        rx, ry = 8 * nx, 8 * ny
        m = jnp.broadcast_to(jnp.sum(ccb[f, k], axis=1, keepdims=True), (nx, 8, 128)).reshape(rx, 128)
        row = iota((rx, 128), 0)
        m = jnp.where(((iota((rx, 128), 1) >> 2) & 1) == (row & 1), m, 0.0)
        hi, lo = split(m)
        out = mm(jnp.concatenate([hi, lo, hi], axis=1), qc[...])
        which = (iota((rx, L), 0) & 7) >> 1
        g = gxb[f, k].reshape(rx, L)
        for i in range(4):
            g = g + jnp.where(which == i, out[:, i * L : (i + 1) * L], 0.0)
        hi, lo = split(g)
        xo[...] = mm(qx[...], jnp.concatenate([hi, lo, hi], axis=0))
        g = gyb[f, k].reshape(ry, L)
        hi = g.astype(BF16).astype(F32)
        lo = g - hi
        pieces = [hi, lo, hi]
        if 3 * ry < L:
            pieces.append(jnp.zeros((L - 3 * ry, L), F32))
        yo[...] = mm(jnp.concatenate(pieces, axis=0).T.astype(BF16), qy[...])

    def y_value(f, r, h):
        cols = slice(h * L, (h + 1) * L)
        re = u_ref[f, pl.ds(r, ROWS), cols] + (yo[pl.ds(r, ROWS), 2 * h * L : (2 * h + 1) * L] + xo[pl.ds(2 * h * L + r, ROWS), :])
        im = u_ref[f, pl.ds(L + r, ROWS), cols] + (yo[pl.ds(r, ROWS), (2 * h + 1) * L : (2 * h + 2) * L] + xo[pl.ds((2 * h + 1) * L + r, ROWS), :])
        return re, im

    def turn(level, r, h, re, im):
        cols = slice(h * L, (h + 1) * L)
        c = cosb[level, pl.ds(r, ROWS), cols]
        s = sinb[level, pl.ds(r, ROWS), cols]
        return re * c - im * s, re * s + im * c

    def source_turn(k):
        def body(r):
            for h in (0, 1):
                cols = slice(h * L, (h + 1) * L)
                re, im = turn(k, r, h, *y_value(0, r, h))
                slev[k + 1, pl.ds(r, ROWS), cols] = re
                slev[k + 1, pl.ds(L + r, ROWS), cols] = im
                put_x(r, h, re, im)

        rows_loop(body)

    def receiver_turn(k):
        level = jnp.maximum(DEPTH - 2 - k, 0)

        def body(r):
            for h in (0, 1):
                cols = slice(h * L, (h + 1) * L)
                re, im = y_value(1, r, h)
                rlev[DEPTH - 1 - k, pl.ds(r, ROWS), cols] = re
                rlev[DEPTH - 1 - k, pl.ds(L + r, ROWS), cols] = im
                put_x(r, h, *turn(level, r, h, re, im))

        rows_loop(body)

    def image_copy(z):
        return pltpu.make_async_copy(imgb.at[z], img_o.at[z], out_sem.at[z])

    def image(z):
        def body(r):
            imgb[z, pl.ds(r, ROWS), :] = (
                slev[z, pl.ds(r, ROWS), :] * rlev[z, pl.ds(r, ROWS), :]
                - slev[z, pl.ds(L + r, ROWS), :] * rlev[z, pl.ds(L + r, ROWS), :]
            )

        rows_loop(body)
        image_copy(z).start()

    ins[0].wait()

    def first_source(r):
        for h in (0, 1):
            cols = slice(h * L, (h + 1) * L)
            put_x(r, h, slev[0, pl.ds(r, ROWS), cols], slev[0, pl.ds(L + r, ROWS), cols])

    rows_loop(first_source)
    pl.semaphore_wait(barrier, nx * ny - 1)
    start(0, 0)
    ins[1].wait()
    ins[2].wait()
    look_up(DEPTH - 1)

    def first_receiver(r):
        for h in (0, 1):
            cols = slice(h * L, (h + 1) * L)
            put_x(r, h, *turn(DEPTH - 1, r, h, rin[pl.ds(r, ROWS), cols], -rin[pl.ds(L + r, ROWS), cols]))

    rows_loop(first_receiver)
    start(1, 0)
    for level in range(DEPTH - 1):
        look_up(level)

    def step(k, carry):
        finish(0, k)
        source_turn(k)

        @pl.when(k < DEPTH - 1)
        def _():
            start(0, k + 1)

        finish(1, k)
        receiver_turn(k)

        @pl.when(k < DEPTH - 1)
        def _():
            start(1, k + 1)

        @pl.when(k == 1)
        def _():
            image(2)

        @pl.when(k == 2)
        def _():
            image(3)
            image(1)

        return carry

    lax.fori_loop(0, DEPTH, step, 0)

    bottom = pltpu.make_async_copy(slev.at[DEPTH], bot_o, out_sem.at[DEPTH])
    bottom.start()

    def flip(r):
        rin[pl.ds(r, ROWS), :] = rlev[0, pl.ds(r, ROWS), :]
        rin[pl.ds(L + r, ROWS), :] = -rlev[0, pl.ds(L + r, ROWS), :]

    rows_loop(flip)
    top = pltpu.make_async_copy(rin, top_o, out_sem.at[DEPTH + 1])
    top.start()
    image(0)
    for f in (0, 1):
        for k in range(DEPTH):
            for kind in range(5):
                arrivals(kind, f, k).wait_send()
    for z in range(DEPTH):
        image_copy(z).wait()
    bottom.wait()
    top.wait()


def solution(mesh):
    nx, ny = mesh.shape["gx"], mesh.shape["gy"]
    rx = 8 * nx

    def on_device(source_field, receiver_field, velocity_index, slowness, freq_index, root_modulus, root_angle):
        width = source_field.shape[3]
        any_spec = pl.BlockSpec(memory_space=pl.ANY)
        smem = pl.BlockSpec(memory_space=pltpu.SMEM)
        vmem = pl.BlockSpec(memory_space=pltpu.VMEM)
        image, bottom, top = pl.pallas_call(
            functools.partial(kernel, nx, ny),
            out_shape=(
                jax.ShapeDtypeStruct((DEPTH, L, width), F32),
                jax.ShapeDtypeStruct((2 * L, width), F32),
                jax.ShapeDtypeStruct((2 * L, width), F32),
            ),
            in_specs=[any_spec, any_spec, any_spec, vmem, smem, smem, smem],
            out_specs=(any_spec, any_spec, any_spec),
            scratch_shapes=[
                pltpu.VMEM((DEPTH + 1, 2 * L, width), F32),
                pltpu.VMEM((DEPTH, 2 * L, width), F32),
                pltpu.VMEM((2 * L, width), F32),
                pltpu.VMEM((DEPTH, L, width), jnp.int32),
                pltpu.VMEM((DEPTH, L, width), F32),
                pltpu.VMEM((DEPTH, L, width), F32),
                pltpu.VMEM((8, 128), F32),
                pltpu.VMEM((2, 2 * L, width), F32),
                pltpu.VMEM((2 * L, width), F32),
                pltpu.VMEM((4 * L, width), BF16),
                pltpu.VMEM((2, L, 4 * L), BF16),
                pltpu.VMEM((4 * L, L), F32),
                pltpu.VMEM((L, 4 * L), F32),
                pltpu.VMEM((DEPTH, L, width), F32),
                pltpu.VMEM((2 * L, 6 * L), BF16),
                pltpu.VMEM((6 * L, 2 * L), BF16),
                pltpu.VMEM((2, 16, 4 * L), BF16),
                pltpu.VMEM((2, L, 3 * L), BF16),
                pltpu.VMEM((4 * L, 3 * rx), BF16),
                pltpu.VMEM((L, 4 * L), BF16),
                pltpu.VMEM((384, 4 * L), BF16),
                pltpu.VMEM((2, DEPTH, nx, 8, L), F32),
                pltpu.VMEM((2, DEPTH, ny, 8, L), F32),
                pltpu.VMEM((2, DEPTH, nx, 8, 128), F32),
                pltpu.SemaphoreType.DMA((3,)),
                pltpu.SemaphoreType.DMA((DEPTH + 2,)),
                pltpu.SemaphoreType.DMA((5, 2, DEPTH)),
                pltpu.SemaphoreType.DMA((5, 2, DEPTH)),
            ],
            compiler_params=pltpu.CompilerParams(collective_id=0, has_side_effects=True, vmem_limit_bytes=56 * 2**20),
        )(
            source_field.reshape(2 * L, width),
            receiver_field.reshape(2 * L, width),
            velocity_index,
            slowness.reshape(1, -1),
            freq_index,
            root_modulus,
            root_angle,
        )
        return image, bottom.reshape(source_field.shape), top.reshape(receiver_field.shape)

    wave = P(None, None, "gx", "gy")
    return jax.shard_map(
        on_device,
        mesh=mesh,
        in_specs=(wave, wave, P(None, "gx", "gy"), P(), P(), P(), P()),
        out_specs=(P(None, "gx", "gy"), wave, wave),
        check_vma=False,
    )
```

```python
import functools

import jax
import jax.numpy as jnp
from jax import lax
from jax.experimental import pallas as pl
from jax.experimental.pallas import tpu as pltpu
from jax.sharding import PartitionSpec as P

MESH = pl.DeviceIdType.MESH
F32 = jnp.float32
BF16 = jnp.bfloat16
L = 256
DEPTH = 4
PHASE_UNIT = 0.05
ROWS = 32


def cmul(a, b):
    return a[0] * b[0] - a[1] * b[1], a[0] * b[1] + a[1] * b[0]


def split(x):
    hi = x.astype(BF16)
    lo = (x - hi.astype(F32)).astype(BF16)
    return hi, lo


def mm(a, b):
    return jnp.dot(a, b, preferred_element_type=F32)


def mm_nt(a, b):
    return lax.dot_general(a, b, (((1,), (1,)), ((), ())), preferred_element_type=F32)


def iota(shape, dim):
    return lax.broadcasted_iota(jnp.int32, shape, dim)


def build_tables(nx, ny, a, b, modulus, angle, va_ref, vb_ref, vl_ref, kw_ref, qx_ref, qy_ref, qc_ref):
    one = jnp.full((8, 128), 1.0, F32)
    m = one * modulus
    th = one * angle
    d = 1.0 - m
    z = d / (2.0 - d)
    z2 = z * z
    logm = -2.0 * z * (1.0 + z2 * (1.0 / 3.0 + z2 * (0.2 + z2 * (1.0 / 7.0 + z2 * (1.0 / 9.0)))))
    ct, st = jnp.cos(th), jnp.sin(th)
    p = (m * ct, m * st)
    kappa = d * (1.0 + m)
    den = (kappa + 2.0 * m * m * st * st, -2.0 * m * m * st * ct)
    inv = 1.0 / (den[0] * den[0] + den[1] * den[1])
    rden = (den[0] * inv, -den[1] * inv)
    gamma = (kappa * kappa * rden[0], kappa * kappa * rden[1])
    beta = (-gamma[0], -gamma[1])
    alpha = cmul((2.0 * kappa * st * st, 2.0 * kappa * st * ct), rden)
    alpha_p = cmul(alpha, p)
    diag = (p[0] * p[0] - p[1] * p[1] + gamma[0], -2.0 * p[0] * p[1] + gamma[1])

    def sc(v):
        return v[0][0:1, 0:1], v[1][0:1, 0:1]

    row = iota((8, L), 0)
    col = iota((8, L), 1)
    expo = jnp.where(row == 0, col, jnp.where(row == 1, L - 1 - col, -col)).astype(F32)
    mag = jnp.exp(expo * logm[0:1, 0:1])
    turn = expo * th[0:1, 0:1]
    pw = (mag * jnp.cos(turn), mag * jnp.sin(turn))
    pw_t = tuple(jnp.concatenate([v] * 16, axis=0).T for v in pw)

    def prow(i):
        return pw[0][i : i + 1, :], pw[1][i : i + 1, :]

    def pcol(i):
        return pw_t[0][:, i : i + 1], pw_t[1][:, i : i + 1]

    h_r, g_r, n_r = prow(0), prow(1), prow(2)
    h_c, g_c, n_c = pcol(0), pcol(1), pcol(2)

    ii = iota((L, L), 0)
    jj = iota((L, L), 1)
    low = ii >= jj
    left = tuple(jnp.where(low, h_c[t], n_c[t]) for t in (0, 1))
    right = tuple(jnp.where(low, n_r[t], h_r[t]) for t in (0, 1))
    k_full = cmul(sc(alpha), cmul(left, right))
    dg = sc(diag)
    k_re = jnp.where(ii == jj, dg[0], k_full[0])
    k_im = jnp.where(ii == jj, dg[1], k_full[1])
    for part, sign_ab in ((k_re, None), (k_im, 1)):
        hi, lo = split(part)
        for which, piece in ((0, hi), (1, lo)):
            if sign_ab is None:
                spots_a = (((0, 0), piece), ((L, L), piece))
                spots_b = spots_a
            else:
                spots_a = (((0, L), -piece), ((L, 0), piece))
                spots_b = (((0, L), piece), ((L, 0), -piece))
            for (r0, c0), val in spots_a:
                if which == 0:
                    va_ref[r0 : r0 + L, c0 : c0 + L] = val
                    va_ref[r0 : r0 + L, 2 * L + c0 : 3 * L + c0] = val
                else:
                    va_ref[r0 : r0 + L, 4 * L + c0 : 5 * L + c0] = val
            for (r0, c0), val in spots_b:
                if which == 0:
                    vb_ref[r0 : r0 + L, c0 : c0 + L] = val
                    vb_ref[2 * L + r0 : 3 * L + r0, c0 : c0 + L] = val
                else:
                    vb_ref[4 * L + r0 : 5 * L + r0, c0 : c0 + L] = val

    r8 = iota((8, L), 0)
    end8 = (r8 & 1) == 1
    v_re = jnp.where(end8, h_r[0], g_r[0])
    v_im = jnp.where(end8, h_r[1], g_r[1])
    imag8 = ((r8 >> 1) & 1) == 1
    v_parts = (jnp.where(imag8, v_im, v_re), jnp.where(imag8, v_re, -v_im))
    for h in (0, 1):
        mine = (r8 >> 2) == h
        for part in (0, 1):
            val = jnp.where(mine, v_parts[part], 0.0)
            hi = val.astype(BF16).astype(F32)
            lo = val - hi
            vl_ref[h, :, part * L : (part + 1) * L] = jnp.concatenate([hi, lo], axis=0).astype(BF16)
            vl_ref[h, :, (2 + part) * L : (3 + part) * L] = jnp.concatenate([hi, jnp.zeros_like(hi)], axis=0).astype(BF16)

    lane = iota((L, 128), 1)
    end_l = ((lane >> 1) & 1) == 1
    imag_l = (lane & 1) == 1
    c_re = jnp.where(end_l, h_c[0], g_c[0])
    c_im = jnp.where(end_l, h_c[1], g_c[1])
    for c0, val in (
        (0, k_re), (L, k_im),
        (2 * L, jnp.where(imag_l, c_im, c_re)),
        (2 * L + 128, jnp.where(imag_l, c_re, -c_im)),
    ):
        hi, lo = split(val)
        kw_ref[0, :, c0 : c0 + val.shape[1]] = hi
        kw_ref[1, :, c0 : c0 + val.shape[1]] = lo

    rr = iota((16, 128), 0)
    kk = iota((16, 128), 1)
    is_x = rr < 2
    is_c = rr >= 6
    target = jnp.where(is_x, a, 2 * b + jnp.where(is_c, (rr - 6) >> 1, (rr - 2) >> 1))
    kk = kk & 63
    source = kk >> 2
    count = jnp.where(is_x, nx, 2 * ny)
    is_s = (rr & 1) == 0
    is_e = jnp.where(is_c, (kk >> 1) & 1, kk & 1) == 1
    is_i = jnp.where(is_c, kk & 1, (kk >> 1) & 1) == 1
    steps = jnp.where(is_s, target - 1 - source, jnp.where(is_e, source - target - 1, 2 * count - 2 - target - source))
    valid = (steps >= 0) & (source < count) & jnp.logical_not(is_s & is_e)
    use_beta = jnp.logical_not(is_s) & jnp.logical_not(is_e)
    n = jnp.maximum(steps, 0).astype(F32)
    th_l = th * float(L)
    wraps = jnp.floor(th_l * 0.15915494309189535 + 0.5)
    th_l = (th_l - wraps * 6.28125) - wraps * 0.0019353071795864769
    mag = jnp.exp(n * (logm[0:1, :] * float(L)))
    om = (mag * jnp.cos(n * th_l[0:1, :]), mag * jnp.sin(n * th_l[0:1, :]))
    coef = tuple(jnp.where(use_beta, beta[t][0:1, :], alpha_p[t][0:1, :]) for t in (0, 1))
    om = cmul(om, coef)
    om = (jnp.where(is_i, -om[1], om[0]), jnp.where(is_i, om[0], om[1]))
    om = tuple(jnp.where(valid, v, 0.0) for v in om)
    om_t = tuple(jnp.concatenate([v] * 8, axis=0).T for v in om)

    first_half = iota((L, 128), 1) < 64
    q1 = cmul(h_c, (om[0][0:1, :], om[1][0:1, :]))
    q2 = cmul(g_c, (om[0][1:2, :], om[1][1:2, :]))
    for part in (0, 1):
        val = q1[part] + q2[part]
        hi = val.astype(BF16).astype(F32)
        qx_ref[part, :, 0:128] = hi.astype(BF16)
        qx_ref[part, :, 128:256] = jnp.where(first_half, val - hi, 0.0).astype(BF16)
    for first, ref in ((2, qy_ref), (6, qc_ref)):
        for h in (0, 1):
            w_s = tuple(om_t[t][:64, first + 2 * h : first + 2 * h + 1] for t in (0, 1))
            w_t = tuple(om_t[t][:64, first + 2 * h + 1 : first + 2 * h + 2] for t in (0, 1))
            q1 = cmul(w_s, h_r)
            q2 = cmul(w_t, g_r)
            for part in (0, 1):
                hi, lo = split(q1[part] + q2[part])
                cols = slice((2 * h + part) * L, (2 * h + part + 1) * L)
                ref[0:64, cols] = hi
                ref[64:128, cols] = hi
                ref[128:192, cols] = lo
        ref[192:256, :] = jnp.zeros((64, 4 * L), BF16)


def kernel(
    nx, ny,
    src, rec, vidx, slow_h, freq, mod, ang,
    img_o, bot_o, top_o,
    slev, rlev, rin, vin, cosb, sinb, tab, u_ref, w_ref, hl, hly, xy, imgb,
    va, vb, vl, kw, qx, qy, qc, gxb, gyb, ccb,
    slow, in_sem, out_sem, send_sem, recv_sem,
):
    a = lax.axis_index("gx")
    b = lax.axis_index("gy")
    ins = [
        pltpu.make_async_copy(src, slev.at[0], in_sem.at[0]),
        pltpu.make_async_copy(rec, rin, in_sem.at[1]),
        pltpu.make_async_copy(vidx, vin, in_sem.at[2]),
        pltpu.make_async_copy(slow_h, slow, in_sem.at[3]),
    ]
    for copy in ins:
        copy.start()

    def ring(i):
        return min(i, 4 - i)

    if nx == 16:
        ax, ay = a // 4, a % 4
        x_peers = [(ring(i) + ring(j), lax.rem(ax + i, 4) * 4 + lax.rem(ay + j, 4)) for i in range(4) for j in range(4) if i or j]
    else:
        x_peers = [(0, lax.rem(a + o, nx)) for o in range(1, nx)]
    y_peers = [(min(o // 2, (ny - o) // 2), lax.rem(b + o, ny)) for o in range(1, ny)]
    peers = [(d, 0, {"gx": p}) for d, p in x_peers] + [(d, 1, {"gy": p}) for d, p in y_peers]
    peers += [(d, 3, {"gx": p}) for d, p in x_peers] + [(d, 4, {"gy": p}) for d, p in y_peers]
    peers += [(d + e, 2, {"gx": p, "gy": q}) for d, p in x_peers for e, q in y_peers]
    peers.sort(key=lambda t: (-t[0], t[1]))

    barrier = pltpu.get_barrier_semaphore()
    for _, kind, peer in peers:
        if kind < 3:
            pl.semaphore_signal(barrier, inc=1, device_id=peer, device_id_type=MESH)

    if ny < 8:
        ccb[...] = jnp.zeros_like(ccb)
    build_tables(nx, ny, a, b, mod[0], ang[0], va, vb, vl, kw, qx, qy, qc)
    ins[3].wait()
    tab[...] = jnp.zeros((8, 128), F32)
    tab[0:1, 0:64] = slow[...]
    rate = jnp.full((8, 128), 1.0, F32) * freq[0].astype(F32) * PHASE_UNIT
    arg = rate * tab[...]
    cos_tab = jnp.broadcast_to(jnp.cos(arg)[0:1, :], (ROWS, 128))
    sin_tab = jnp.broadcast_to(jnp.sin(arg)[0:1, :], (ROWS, 128))

    def rows_loop(body):
        def go(i, carry):
            body(pl.multiple_of(i * ROWS, ROWS))
            return carry

        lax.fori_loop(0, L // ROWS, go, 0)

    def look_up(level):
        def body(r):
            for c in range(4):
                idx = vin[level, pl.ds(r, ROWS), c * 128 : (c + 1) * 128]
                cosb[level, pl.ds(r, ROWS), c * 128 : (c + 1) * 128] = jnp.take_along_axis(cos_tab, idx, axis=1, mode="promise_in_bounds")
                sinb[level, pl.ds(r, ROWS), c * 128 : (c + 1) * 128] = jnp.take_along_axis(sin_tab, idx, axis=1, mode="promise_in_bounds")

        rows_loop(body)

    def put_x(r, h, re, im):
        cols = slice(h * L, (h + 1) * L)
        for part, val in ((0, re), (1, im)):
            hi, lo = split(val)
            hl[pl.ds(part * L + r, ROWS), cols] = hi
            hl[pl.ds((2 + part) * L + r, ROWS), cols] = lo
            hl[pl.ds((4 + part) * L + r, ROWS), cols] = hi

    def slot(kind, f, k):
        if kind == 0:
            return gxb.at[f, k, a]
        if kind == 1:
            return gyb.at[f, k, b]
        return ccb.at[f, k, a, pl.ds(b, 1)]

    def arrivals(kind, f, k):
        block = (
            gxb.at[f, k, pl.ds(0, nx - 1)],
            gyb.at[f, k, pl.ds(0, ny - 1)],
            ccb.at[f, k, pl.ds(0, nx - 1), pl.ds(0, ny - 1)],
            ccb.at[f, k, pl.ds(0, nx - 1), pl.ds(0, 1)],
            ccb.at[f, k, 0, pl.ds(0, ny - 1)],
        )[kind]
        return pltpu.make_async_remote_copy(block, block, send_sem.at[kind, f, k], recv_sem.at[kind, f, k], device_id={"gx": a}, device_id_type=MESH)

    real8 = ((iota((8, L), 0) >> 1) & 1) == 0
    lane8, row8 = iota((8, 128), 1), iota((8, 128), 0)
    corner_mask = (((row8 >> 1) & 1) == 0) & ((lane8 >> 6) == (row8 & 1)) & (((lane8 >> 2) & 1) == (row8 >> 2)) & (((lane8 >> 3) & 7) == b)

    def times_i(q):
        return jnp.where(real8, -pltpu.roll(q, 6, 0), pltpu.roll(q, 2, 0))

    def local(f):
        w_ref[...] = mm(va[...], hl[...])

        def body(r):
            for h in (0, 1):
                for part in (0, 1):
                    hi, lo = split(w_ref[pl.ds(part * L + r, ROWS), h * L : (h + 1) * L])
                    hly[pl.ds(h * L + r, ROWS), part * L : (part + 1) * L] = hi
                    hly[pl.ds(h * L + r, ROWS), (2 + part) * L : (3 + part) * L] = lo
                    hly[pl.ds(h * L + r, ROWS), (4 + part) * L : (5 + part) * L] = hi

        rows_loop(body)
        u_ref[f] = mm(hly[...], vb[...])

    def carry(f, k):
        acc_x = acc_y = jnp.zeros((16, L), F32)
        for h in (0, 1):
            cols = slice(h * L, (h + 1) * L)
            acc_x = acc_x + mm(vl[h], hl[0 : 4 * L, cols])
            for i in range(4):
                acc_y = acc_y + mm_nt(vl[h, :, i * L : (i + 1) * L], hl[i * L : (i + 1) * L, cols])
        carries = jnp.concatenate([acc_x[0:8] + acc_x[8:16], acc_y[0:8] + acc_y[8:16]], axis=0)
        hi = carries.astype(BF16).astype(F32)
        both = jnp.concatenate([hi, carries - hi], axis=0).astype(BF16)
        out = mm(both, kw[0])
        out = out[0:16] + out[16:32] + mm(both[0:16], kw[1])
        gxb[f, k, a] = out[0:8, 0:L] + times_i(out[0:8, L : 2 * L])
        gyb[f, k, b] = out[8:16, 0:L] + times_i(out[8:16, L : 2 * L])
        corner = out[0:8, 2 * L : 2 * L + 128] + pltpu.roll(out[0:8, 2 * L + 128 : 3 * L], 6, 0)
        ccb[f, k, a, pl.ds(b, 1)] = jnp.sum(jnp.where(corner_mask, corner, 0.0), axis=0, keepdims=True)
    def send(f, k):
        for _, kind, peer in peers:
            here = slot(kind, f, k)
            pltpu.make_async_remote_copy(here, here, send_sem.at[kind, f, k], recv_sem.at[kind, f, k], device_id=peer, device_id_type=MESH).start()

    def start(f, k):
        carry(f, k)
        send(f, k)
        local(f)

    def finish(f, k):
        for kind in range(5):
            arrivals(kind, f, k).wait_recv()
        pairs = nx // 2
        m = jnp.sum(ccb[f, k], axis=1, keepdims=True).reshape(pairs, 2, 1, 128)
        shape = (pairs, 8, 128)
        m = jnp.where(iota(shape, 1) < 4, jnp.broadcast_to(m[:, 0], shape), jnp.broadcast_to(m[:, 1], shape)).reshape(4 * nx, 128)
        left = iota((4 * nx, 128), 1) < 64
        row = iota((4 * nx, 128), 0)
        m = jnp.where((row & 1) == 1, pltpu.roll(m, 64, 1), m)
        hi = m.astype(BF16).astype(F32)
        m = jnp.concatenate([jnp.where(left, hi, pltpu.roll(m - hi, 64, 1)), jnp.where(left, hi, 0.0)], axis=1).astype(BF16)
        corr = mm(m, qc[...])
        real = ((iota((4 * nx, L), 0) >> 1) & 1) == 0
        g = gxb[f, k].reshape(pairs, 2, 8, L)
        even, odd = g[:, 0], g[:, 1]
        top = iota((pairs, 8, L), 1) < 4
        g = (jnp.where(top, even, pltpu.roll(odd, 4, 1)), jnp.where(top, pltpu.roll(even, 4, 1), odd))
        gx3 = []
        for h in (0, 1):
            val = g[h].reshape(4 * nx, L) + jnp.where(real, corr[:, 2 * h * L : (2 * h + 1) * L], corr[:, (2 * h + 1) * L : (2 * h + 2) * L])
            hi, lo = split(val)
            pad = jnp.zeros((64 - 4 * nx, L), BF16)
            fill = [pad] if 4 * nx < 64 else []
            gx3.append(jnp.concatenate([hi] + fill + [lo] + fill + [hi] + fill + [jnp.zeros((64, L), BF16)], axis=0))
        gy = gyb[f, k].reshape(8 * ny, L)
        hi = gy.astype(BF16).astype(F32)
        fill = [jnp.zeros((64 - 8 * ny, L), F32)] if 8 * ny < 64 else []
        gy3 = jnp.concatenate([hi] + fill + [gy - hi] + fill + [hi] + fill + [jnp.zeros((64, L), F32)], axis=0).T.astype(BF16)
        for h in (0, 1):
            for part in (0, 1):
                i = 2 * h + part
                xy[i * L : (i + 1) * L, :] = mm(qx[part], gx3[h]) + mm(gy3, qy[:, i * L : (i + 1) * L])

    def y_value(f, r, h):
        re = u_ref[f, pl.ds(h * L + r, ROWS), 0:L] + xy[pl.ds(2 * h * L + r, ROWS), :]
        im = u_ref[f, pl.ds(h * L + r, ROWS), L : 2 * L] + xy[pl.ds((2 * h + 1) * L + r, ROWS), :]
        return re, im

    def turn(level, r, h, re, im):
        cols = slice(h * L, (h + 1) * L)
        c = cosb[level, pl.ds(r, ROWS), cols]
        s = sinb[level, pl.ds(r, ROWS), cols]
        return re * c - im * s, re * s + im * c

    def source_turn(k):
        def body(r):
            for h in (0, 1):
                cols = slice(h * L, (h + 1) * L)
                re, im = turn(k, r, h, *y_value(0, r, h))
                slev[k + 1, pl.ds(r, ROWS), cols] = re
                slev[k + 1, pl.ds(L + r, ROWS), cols] = im
                put_x(r, h, re, im)

        rows_loop(body)

    def receiver_turn(k):
        level = jnp.maximum(DEPTH - 2 - k, 0)

        def body(r):
            for h in (0, 1):
                cols = slice(h * L, (h + 1) * L)
                re, im = y_value(1, r, h)
                rlev[DEPTH - 1 - k, pl.ds(r, ROWS), cols] = re
                rlev[DEPTH - 1 - k, pl.ds(L + r, ROWS), cols] = im
                put_x(r, h, *turn(level, r, h, re, im))

        rows_loop(body)

    def image_copy(z):
        return pltpu.make_async_copy(imgb.at[z], img_o.at[z], out_sem.at[z])

    def image(z):
        def body(r):
            imgb[z, pl.ds(r, ROWS), :] = (
                slev[z, pl.ds(r, ROWS), :] * rlev[z, pl.ds(r, ROWS), :]
                - slev[z, pl.ds(L + r, ROWS), :] * rlev[z, pl.ds(L + r, ROWS), :]
            )

        rows_loop(body)
        image_copy(z).start()

    ins[0].wait()

    def first_source(r):
        for h in (0, 1):
            cols = slice(h * L, (h + 1) * L)
            put_x(r, h, slev[0, pl.ds(r, ROWS), cols], slev[0, pl.ds(L + r, ROWS), cols])

    rows_loop(first_source)
    carry(0, 0)
    ins[2].wait()
    for level in (DEPTH - 1, 0, DEPTH - 2):
        look_up(level)
    ins[1].wait()
    pl.semaphore_wait(barrier, nx * ny - 1)
    send(0, 0)
    local(0)

    def first_receiver(r):
        for h in (0, 1):
            cols = slice(h * L, (h + 1) * L)
            put_x(r, h, *turn(DEPTH - 1, r, h, rin[pl.ds(r, ROWS), cols], -rin[pl.ds(L + r, ROWS), cols]))

    rows_loop(first_receiver)
    start(1, 0)
    for level in range(1, DEPTH - 2):
        look_up(level)

    def step(k, state):
        finish(0, k)
        source_turn(k)
        start(0, k + 1)
        finish(1, k)
        receiver_turn(k)
        start(1, k + 1)

        @pl.when(k == 1)
        def _():
            image(2)

        @pl.when(k == 2)
        def _():
            image(3)
            image(1)

        return state

    lax.fori_loop(0, DEPTH - 1, step, 0)

    def last_source(r):
        for h in (0, 1):
            cols = slice(h * L, (h + 1) * L)
            re, im = turn(DEPTH - 1, r, h, *y_value(0, r, h))
            slev[DEPTH, pl.ds(r, ROWS), cols] = re
            slev[DEPTH, pl.ds(L + r, ROWS), cols] = im

    def last_receiver(r):
        for h in (0, 1):
            cols = slice(h * L, (h + 1) * L)
            re, im = y_value(1, r, h)
            rin[pl.ds(r, ROWS), cols] = re
            rin[pl.ds(L + r, ROWS), cols] = -im
            imgb[0, pl.ds(r, ROWS), cols] = slev[0, pl.ds(r, ROWS), cols] * re - slev[0, pl.ds(L + r, ROWS), cols] * im

    finish(0, DEPTH - 1)
    rows_loop(last_source)
    bottom = pltpu.make_async_copy(slev.at[DEPTH], bot_o, out_sem.at[DEPTH])
    bottom.start()
    finish(1, DEPTH - 1)
    rows_loop(last_receiver)
    image_copy(0).start()
    top = pltpu.make_async_copy(rin, top_o, out_sem.at[DEPTH + 1])
    top.start()
    for f in (0, 1):
        for k in range(DEPTH):
            for kind in range(5):
                arrivals(kind, f, k).wait_send()
    for z in range(DEPTH):
        image_copy(z).wait()
    bottom.wait()
    top.wait()


def write_out(image, bottom, top, image_o, bottom_o, top_o, sem):
    copies = [pltpu.make_async_copy(v, o, sem.at[i]) for i, (v, o) in enumerate(((image, image_o), (bottom, bottom_o), (top, top_o)))]
    for copy in copies:
        copy.start()
    for copy in copies:
        copy.wait()


def solution(mesh):
    nx, ny = mesh.shape["gx"], mesh.shape["gy"]

    def on_device(source_field, receiver_field, velocity_index, slowness, freq_index, root_modulus, root_angle):
        width = source_field.shape[3]
        any_spec = pl.BlockSpec(memory_space=pl.ANY)
        hbm = pl.BlockSpec(memory_space=pltpu.HBM)
        smem = pl.BlockSpec(memory_space=pltpu.SMEM)
        image, bottom, top = pl.pallas_call(
            functools.partial(kernel, nx, ny),
            out_shape=(
                jax.ShapeDtypeStruct((DEPTH, L, width), F32),
                jax.ShapeDtypeStruct((2 * L, width), F32),
                jax.ShapeDtypeStruct((2 * L, width), F32),
            ),
            in_specs=[hbm] * 4 + [smem] * 3,
            out_specs=(any_spec, any_spec, any_spec),
            scratch_shapes=[
                pltpu.VMEM((DEPTH + 1, 2 * L, width), F32),
                pltpu.VMEM((DEPTH, 2 * L, width), F32),
                pltpu.VMEM((2 * L, width), F32),
                pltpu.VMEM((DEPTH, L, width), jnp.int32),
                pltpu.VMEM((DEPTH, L, width), F32),
                pltpu.VMEM((DEPTH, L, width), F32),
                pltpu.VMEM((8, 128), F32),
                pltpu.VMEM((2, 2 * L, width), F32),
                pltpu.VMEM((2 * L, width), F32),
                pltpu.VMEM((6 * L, width), BF16),
                pltpu.VMEM((2 * L, 6 * L), BF16),
                pltpu.VMEM((4 * L, L), F32),
                pltpu.VMEM((DEPTH, L, width), F32),
                pltpu.VMEM((2 * L, 6 * L), BF16),
                pltpu.VMEM((6 * L, 2 * L), BF16),
                pltpu.VMEM((2, 16, 4 * L), BF16),
                pltpu.VMEM((2, L, 3 * L), BF16),
                pltpu.VMEM((2, L, L), BF16),
                pltpu.VMEM((L, 4 * L), BF16),
                pltpu.VMEM((L, 4 * L), BF16),
                pltpu.VMEM((2, DEPTH, nx, 8, L), F32),
                pltpu.VMEM((2, DEPTH, ny, 8, L), F32),
                pltpu.VMEM((2, DEPTH, nx, 8, 128), F32),
                pltpu.VMEM((1, 64), F32),
                pltpu.SemaphoreType.DMA((4,)),
                pltpu.SemaphoreType.DMA((DEPTH + 2,)),
                pltpu.SemaphoreType.DMA((5, 2, DEPTH)),
                pltpu.SemaphoreType.DMA((5, 2, DEPTH)),
            ],
            compiler_params=pltpu.CompilerParams(collective_id=0, has_side_effects=True, vmem_limit_bytes=44 * 2**20),
        )(
            pltpu.with_memory_space_constraint(source_field.reshape(2 * L, width), pltpu.HBM),
            pltpu.with_memory_space_constraint(receiver_field.reshape(2 * L, width), pltpu.HBM),
            pltpu.with_memory_space_constraint(velocity_index, pltpu.HBM),
            pltpu.with_memory_space_constraint(slowness.reshape(1, -1), pltpu.HBM),
            freq_index,
            root_modulus,
            root_angle,
        )
        image, bottom, top = pl.pallas_call(
            write_out,
            out_shape=tuple(jax.ShapeDtypeStruct(v.shape, F32) for v in (image, bottom, top)),
            in_specs=[any_spec] * 3,
            out_specs=(any_spec,) * 3,
            scratch_shapes=[pltpu.SemaphoreType.DMA((3,))],
            compiler_params=pltpu.CompilerParams(vmem_limit_bytes=2**20),
        )(image, bottom, top)
        return image, bottom.reshape(source_field.shape), top.reshape(receiver_field.shape)

    wave = P(None, None, "gx", "gy")
    return jax.shard_map(
        on_device,
        mesh=mesh,
        in_specs=(wave, wave, P(None, "gx", "gy"), P(), P(), P(), P()),
        out_specs=(P(None, "gx", "gy"), wave, wave),
        check_vma=False,
    )
```

```python
import functools

import jax
import jax.numpy as jnp
from jax import lax
from jax.experimental import pallas as pl
from jax.experimental.pallas import tpu as pltpu
from jax.sharding import PartitionSpec as P

MESH = pl.DeviceIdType.MESH
F32 = jnp.float32
BF16 = jnp.bfloat16
L = 256
DEPTH = 4
PHASE_UNIT = 0.05
ROWS = 32


def cmul(a, b):
    return a[0] * b[0] - a[1] * b[1], a[0] * b[1] + a[1] * b[0]


def split(x):
    hi = x.astype(BF16)
    lo = (x - hi.astype(F32)).astype(BF16)
    return hi, lo


def mm(a, b):
    return jnp.dot(a, b, preferred_element_type=F32)


def mm_nt(a, b):
    return lax.dot_general(a, b, (((1,), (1,)), ((), ())), preferred_element_type=F32)


def iota(shape, dim):
    return lax.broadcasted_iota(jnp.int32, shape, dim)


def build_tables(nx, ny, a, b, modulus, angle, va_ref, vb_ref, vl_ref, kw_ref, qx_ref, qy_ref, qc_ref):
    one = jnp.full((8, 128), 1.0, F32)
    m = one * modulus
    th = one * angle
    d = 1.0 - m
    z = d / (2.0 - d)
    z2 = z * z
    logm = -2.0 * z * (1.0 + z2 * (1.0 / 3.0 + z2 * (0.2 + z2 * (1.0 / 7.0 + z2 * (1.0 / 9.0)))))
    ct, st = jnp.cos(th), jnp.sin(th)
    p = (m * ct, m * st)
    kappa = d * (1.0 + m)
    den = (kappa + 2.0 * m * m * st * st, -2.0 * m * m * st * ct)
    inv = 1.0 / (den[0] * den[0] + den[1] * den[1])
    rden = (den[0] * inv, -den[1] * inv)
    gamma = (kappa * kappa * rden[0], kappa * kappa * rden[1])
    beta = (-gamma[0], -gamma[1])
    alpha = cmul((2.0 * kappa * st * st, 2.0 * kappa * st * ct), rden)
    alpha_p = cmul(alpha, p)
    diag = (p[0] * p[0] - p[1] * p[1] + gamma[0], -2.0 * p[0] * p[1] + gamma[1])

    def sc(v):
        return v[0][0:1, 0:1], v[1][0:1, 0:1]

    row = iota((8, L), 0)
    col = iota((8, L), 1)
    expo = jnp.where(row == 0, col, jnp.where(row == 1, L - 1 - col, -col)).astype(F32)
    mag = jnp.exp(expo * logm[0:1, 0:1])
    turn = expo * th[0:1, 0:1]
    pw = (mag * jnp.cos(turn), mag * jnp.sin(turn))
    pw_t = tuple(jnp.concatenate([v] * 16, axis=0).T for v in pw)

    def prow(i):
        return pw[0][i : i + 1, :], pw[1][i : i + 1, :]

    def pcol(i):
        return pw_t[0][:, i : i + 1], pw_t[1][:, i : i + 1]

    h_r, g_r, n_r = prow(0), prow(1), prow(2)
    h_c, g_c, n_c = pcol(0), pcol(1), pcol(2)

    ii = iota((L, L), 0)
    jj = iota((L, L), 1)
    low = ii >= jj
    left = tuple(jnp.where(low, h_c[t], n_c[t]) for t in (0, 1))
    right = tuple(jnp.where(low, n_r[t], h_r[t]) for t in (0, 1))
    k_full = cmul(sc(alpha), cmul(left, right))
    dg = sc(diag)
    k_re = jnp.where(ii == jj, dg[0], k_full[0])
    k_im = jnp.where(ii == jj, dg[1], k_full[1])
    for part, sign_ab in ((k_re, None), (k_im, 1)):
        hi, lo = split(part)
        for which, piece in ((0, hi), (1, lo)):
            if sign_ab is None:
                spots_a = (((0, 0), piece), ((L, L), piece))
                spots_b = spots_a
            else:
                spots_a = (((0, L), -piece), ((L, 0), piece))
                spots_b = (((0, L), piece), ((L, 0), -piece))
            for (r0, c0), val in spots_a:
                if which == 0:
                    va_ref[r0 : r0 + L, c0 : c0 + L] = val
                    va_ref[r0 : r0 + L, 2 * L + c0 : 3 * L + c0] = val
                else:
                    va_ref[r0 : r0 + L, 4 * L + c0 : 5 * L + c0] = val
            for (r0, c0), val in spots_b:
                if which == 0:
                    vb_ref[r0 : r0 + L, c0 : c0 + L] = val
                    vb_ref[2 * L + r0 : 3 * L + r0, c0 : c0 + L] = val
                else:
                    vb_ref[4 * L + r0 : 5 * L + r0, c0 : c0 + L] = val

    r8 = iota((8, L), 0)
    end8 = (r8 & 1) == 1
    v_re = jnp.where(end8, h_r[0], g_r[0])
    v_im = jnp.where(end8, h_r[1], g_r[1])
    imag8 = ((r8 >> 1) & 1) == 1
    v_parts = (jnp.where(imag8, v_im, v_re), jnp.where(imag8, v_re, -v_im))
    for h in (0, 1):
        mine = (r8 >> 2) == h
        for part in (0, 1):
            val = jnp.where(mine, v_parts[part], 0.0)
            hi = val.astype(BF16).astype(F32)
            lo = val - hi
            vl_ref[h, :, part * L : (part + 1) * L] = jnp.concatenate([hi, lo], axis=0).astype(BF16)
            vl_ref[h, :, (2 + part) * L : (3 + part) * L] = jnp.concatenate([hi, jnp.zeros_like(hi)], axis=0).astype(BF16)

    lane = iota((L, 128), 1)
    end_l = ((lane >> 1) & 1) == 1
    imag_l = (lane & 1) == 1
    c_re = jnp.where(end_l, h_c[0], g_c[0])
    c_im = jnp.where(end_l, h_c[1], g_c[1])
    for c0, val in (
        (0, k_re), (L, k_im),
        (2 * L, jnp.where(imag_l, c_im, c_re)),
        (2 * L + 128, jnp.where(imag_l, c_re, -c_im)),
    ):
        hi, lo = split(val)
        kw_ref[0, :, c0 : c0 + val.shape[1]] = hi
        kw_ref[1, :, c0 : c0 + val.shape[1]] = lo

    rr = iota((16, 128), 0)
    kk = iota((16, 128), 1)
    is_x = rr < 2
    is_c = rr >= 6
    target = jnp.where(is_x, a, 2 * b + jnp.where(is_c, (rr - 6) >> 1, (rr - 2) >> 1))
    kk = kk & 63
    source = kk >> 2
    count = jnp.where(is_x, nx, 2 * ny)
    is_s = (rr & 1) == 0
    is_e = jnp.where(is_c, (kk >> 1) & 1, kk & 1) == 1
    is_i = jnp.where(is_c, kk & 1, (kk >> 1) & 1) == 1
    steps = jnp.where(is_s, target - 1 - source, jnp.where(is_e, source - target - 1, 2 * count - 2 - target - source))
    valid = (steps >= 0) & (source < count) & jnp.logical_not(is_s & is_e)
    use_beta = jnp.logical_not(is_s) & jnp.logical_not(is_e)
    n = jnp.maximum(steps, 0).astype(F32)
    th_l = th * float(L)
    wraps = jnp.floor(th_l * 0.15915494309189535 + 0.5)
    th_l = (th_l - wraps * 6.28125) - wraps * 0.0019353071795864769
    mag = jnp.exp(n * (logm[0:1, :] * float(L)))
    om = (mag * jnp.cos(n * th_l[0:1, :]), mag * jnp.sin(n * th_l[0:1, :]))
    coef = tuple(jnp.where(use_beta, beta[t][0:1, :], alpha_p[t][0:1, :]) for t in (0, 1))
    om = cmul(om, coef)
    om = (jnp.where(is_i, -om[1], om[0]), jnp.where(is_i, om[0], om[1]))
    om = tuple(jnp.where(valid, v, 0.0) for v in om)
    om_t = tuple(jnp.concatenate([v] * 8, axis=0).T for v in om)

    first_half = iota((L, 128), 1) < 64
    q1 = cmul(h_c, (om[0][0:1, :], om[1][0:1, :]))
    q2 = cmul(g_c, (om[0][1:2, :], om[1][1:2, :]))
    for part in (0, 1):
        val = q1[part] + q2[part]
        hi = val.astype(BF16).astype(F32)
        qx_ref[part, :, 0:128] = hi.astype(BF16)
        qx_ref[part, :, 128:256] = jnp.where(first_half, val - hi, 0.0).astype(BF16)
    for first, ref in ((2, qy_ref), (6, qc_ref)):
        for h in (0, 1):
            w_s = tuple(om_t[t][:64, first + 2 * h : first + 2 * h + 1] for t in (0, 1))
            w_t = tuple(om_t[t][:64, first + 2 * h + 1 : first + 2 * h + 2] for t in (0, 1))
            q1 = cmul(w_s, h_r)
            q2 = cmul(w_t, g_r)
            for part in (0, 1):
                hi, lo = split(q1[part] + q2[part])
                cols = slice((2 * h + part) * L, (2 * h + part + 1) * L)
                ref[0:64, cols] = hi
                ref[64:128, cols] = hi
                ref[128:192, cols] = lo
        ref[192:256, :] = jnp.zeros((64, 4 * L), BF16)


def kernel(
    nx, ny,
    src, rec, vidx, slow_h, freq, mod, ang,
    img_o, bot_o, top_o,
    slev, rlev, rin, vin, cosb, sinb, tab, u_ref, w_ref, hl, hly, xy,
    va, vb, vl, kw, qx, qy, qc, gxb, gyb, ccb,
    slow, in_sem, send_sem, recv_sem,
):
    a = lax.axis_index("gx")
    b = lax.axis_index("gy")
    ins = [
        pltpu.make_async_copy(src, slev.at[0], in_sem.at[0]),
        pltpu.make_async_copy(rec, rin, in_sem.at[1]),
        pltpu.make_async_copy(vidx, vin, in_sem.at[2]),
        pltpu.make_async_copy(slow_h, slow, in_sem.at[3]),
    ]
    for copy in ins:
        copy.start()

    def ring(i):
        return min(i, 4 - i)

    if nx == 16:
        ax, ay = a // 4, a % 4
        x_peers = [(ring(i) + ring(j), lax.rem(ax + i, 4) * 4 + lax.rem(ay + j, 4)) for i in range(4) for j in range(4) if i or j]
    else:
        x_peers = [(0, lax.rem(a + o, nx)) for o in range(1, nx)]
    y_peers = [(min(o // 2, (ny - o) // 2), lax.rem(b + o, ny)) for o in range(1, ny)]
    peers = [(d, 0, {"gx": p}) for d, p in x_peers] + [(d, 1, {"gy": p}) for d, p in y_peers]
    peers += [(d, 3, {"gx": p}) for d, p in x_peers] + [(d, 4, {"gy": p}) for d, p in y_peers]
    peers += [(d + e, 2, {"gx": p, "gy": q}) for d, p in x_peers for e, q in y_peers]
    peers.sort(key=lambda t: (-t[0], t[1]))

    barrier = pltpu.get_barrier_semaphore()
    for _, kind, peer in peers:
        if kind < 3:
            pl.semaphore_signal(barrier, inc=1, device_id=peer, device_id_type=MESH)

    if ny < 8:
        ccb[...] = jnp.zeros_like(ccb)
    build_tables(nx, ny, a, b, mod[0], ang[0], va, vb, vl, kw, qx, qy, qc)
    ins[3].wait()
    tab[...] = jnp.zeros((8, 128), F32)
    tab[0:1, 0:64] = slow[...]
    rate = jnp.full((8, 128), 1.0, F32) * freq[0].astype(F32) * PHASE_UNIT
    arg = rate * tab[...]
    cos_tab = jnp.broadcast_to(jnp.cos(arg)[0:1, :], (ROWS, 128))
    sin_tab = jnp.broadcast_to(jnp.sin(arg)[0:1, :], (ROWS, 128))

    def rows_loop(body):
        def go(i, carry):
            body(pl.multiple_of(i * ROWS, ROWS))
            return carry

        lax.fori_loop(0, L // ROWS, go, 0)

    def look_up(level):
        def body(r):
            for c in range(4):
                idx = vin[level, pl.ds(r, ROWS), c * 128 : (c + 1) * 128]
                cosb[level, pl.ds(r, ROWS), c * 128 : (c + 1) * 128] = jnp.take_along_axis(cos_tab, idx, axis=1, mode="promise_in_bounds")
                sinb[level, pl.ds(r, ROWS), c * 128 : (c + 1) * 128] = jnp.take_along_axis(sin_tab, idx, axis=1, mode="promise_in_bounds")

        rows_loop(body)

    def put_x(r, h, re, im):
        cols = slice(h * L, (h + 1) * L)
        for part, val in ((0, re), (1, im)):
            hi, lo = split(val)
            hl[pl.ds(part * L + r, ROWS), cols] = hi
            hl[pl.ds((2 + part) * L + r, ROWS), cols] = lo
            hl[pl.ds((4 + part) * L + r, ROWS), cols] = hi

    def slot(kind, f, k):
        if kind == 0:
            return gxb.at[f, k, a]
        if kind == 1:
            return gyb.at[f, k, b]
        return ccb.at[f, k, a, pl.ds(b, 1)]

    def arrivals(kind, f, k):
        block = (
            gxb.at[f, k, pl.ds(0, nx - 1)],
            gyb.at[f, k, pl.ds(0, ny - 1)],
            ccb.at[f, k, pl.ds(0, nx - 1), pl.ds(0, ny - 1)],
            ccb.at[f, k, pl.ds(0, nx - 1), pl.ds(0, 1)],
            ccb.at[f, k, 0, pl.ds(0, ny - 1)],
        )[kind]
        return pltpu.make_async_remote_copy(block, block, send_sem.at[kind, f, k], recv_sem.at[kind, f, k], device_id={"gx": a}, device_id_type=MESH)

    real8 = ((iota((8, L), 0) >> 1) & 1) == 0
    lane8, row8 = iota((8, 128), 1), iota((8, 128), 0)
    corner_mask = (((row8 >> 1) & 1) == 0) & ((lane8 >> 6) == (row8 & 1)) & (((lane8 >> 2) & 1) == (row8 >> 2)) & (((lane8 >> 3) & 7) == b)

    def times_i(q):
        return jnp.where(real8, -pltpu.roll(q, 6, 0), pltpu.roll(q, 2, 0))

    def local(f):
        w_ref[...] = mm(va[...], hl[...])

        def body(r):
            for h in (0, 1):
                for part in (0, 1):
                    hi, lo = split(w_ref[pl.ds(part * L + r, ROWS), h * L : (h + 1) * L])
                    hly[pl.ds(h * L + r, ROWS), part * L : (part + 1) * L] = hi
                    hly[pl.ds(h * L + r, ROWS), (2 + part) * L : (3 + part) * L] = lo
                    hly[pl.ds(h * L + r, ROWS), (4 + part) * L : (5 + part) * L] = hi

        rows_loop(body)
        u_ref[f] = mm(hly[...], vb[...])

    def carry(f, k):
        acc_x = acc_y = jnp.zeros((16, L), F32)
        for h in (0, 1):
            cols = slice(h * L, (h + 1) * L)
            acc_x = acc_x + mm(vl[h], hl[0 : 4 * L, cols])
            for i in range(4):
                acc_y = acc_y + mm_nt(vl[h, :, i * L : (i + 1) * L], hl[i * L : (i + 1) * L, cols])
        carries = jnp.concatenate([acc_x[0:8] + acc_x[8:16], acc_y[0:8] + acc_y[8:16]], axis=0)
        hi = carries.astype(BF16).astype(F32)
        both = jnp.concatenate([hi, carries - hi], axis=0).astype(BF16)
        out = mm(both, kw[0])
        out = out[0:16] + out[16:32] + mm(both[0:16], kw[1])
        gxb[f, k, a] = out[0:8, 0:L] + times_i(out[0:8, L : 2 * L])
        gyb[f, k, b] = out[8:16, 0:L] + times_i(out[8:16, L : 2 * L])
        corner = out[0:8, 2 * L : 2 * L + 128] + pltpu.roll(out[0:8, 2 * L + 128 : 3 * L], 6, 0)
        ccb[f, k, a, pl.ds(b, 1)] = jnp.sum(jnp.where(corner_mask, corner, 0.0), axis=0, keepdims=True)
    def send(f, k):
        for _, kind, peer in peers:
            here = slot(kind, f, k)
            pltpu.make_async_remote_copy(here, here, send_sem.at[kind, f, k], recv_sem.at[kind, f, k], device_id=peer, device_id_type=MESH).start()

    def start(f, k):
        carry(f, k)
        send(f, k)
        pl.when(a < nx)(lambda: local(f))

    def finish(f, k):
        for kind in range(5):
            arrivals(kind, f, k).wait_recv()
        pairs = nx // 2
        m = jnp.sum(ccb[f, k], axis=1, keepdims=True).reshape(pairs, 2, 1, 128)
        shape = (pairs, 8, 128)
        m = jnp.where(iota(shape, 1) < 4, jnp.broadcast_to(m[:, 0], shape), jnp.broadcast_to(m[:, 1], shape)).reshape(4 * nx, 128)
        left = iota((4 * nx, 128), 1) < 64
        row = iota((4 * nx, 128), 0)
        m = jnp.where((row & 1) == 1, pltpu.roll(m, 64, 1), m)
        hi = m.astype(BF16).astype(F32)
        m = jnp.concatenate([jnp.where(left, hi, pltpu.roll(m - hi, 64, 1)), jnp.where(left, hi, 0.0)], axis=1).astype(BF16)
        corr = mm(m, qc[...])
        real = ((iota((4 * nx, L), 0) >> 1) & 1) == 0
        g = gxb[f, k].reshape(pairs, 2, 8, L)
        even, odd = g[:, 0], g[:, 1]
        top = iota((pairs, 8, L), 1) < 4
        g = (jnp.where(top, even, pltpu.roll(odd, 4, 1)), jnp.where(top, pltpu.roll(even, 4, 1), odd))
        gx3 = []
        for h in (0, 1):
            val = g[h].reshape(4 * nx, L) + jnp.where(real, corr[:, 2 * h * L : (2 * h + 1) * L], corr[:, (2 * h + 1) * L : (2 * h + 2) * L])
            hi, lo = split(val)
            pad = jnp.zeros((64 - 4 * nx, L), BF16)
            fill = [pad] if 4 * nx < 64 else []
            gx3.append(jnp.concatenate([hi] + fill + [lo] + fill + [hi] + fill + [jnp.zeros((64, L), BF16)], axis=0))
        gy = gyb[f, k].reshape(8 * ny, L)
        hi = gy.astype(BF16).astype(F32)
        fill = [jnp.zeros((64 - 8 * ny, L), F32)] if 8 * ny < 64 else []
        gy3 = jnp.concatenate([hi] + fill + [gy - hi] + fill + [hi] + fill + [jnp.zeros((64, L), F32)], axis=0).T.astype(BF16)
        for h in (0, 1):
            for part in (0, 1):
                i = 2 * h + part
                xy[i * L : (i + 1) * L, :] = mm(qx[part], gx3[h]) + mm(gy3, qy[:, i * L : (i + 1) * L])

    def y_value(f, r, h):
        re = u_ref[f, pl.ds(h * L + r, ROWS), 0:L] + xy[pl.ds(2 * h * L + r, ROWS), :]
        im = u_ref[f, pl.ds(h * L + r, ROWS), L : 2 * L] + xy[pl.ds((2 * h + 1) * L + r, ROWS), :]
        return re, im

    def turn(level, r, h, re, im):
        cols = slice(h * L, (h + 1) * L)
        c = cosb[level, pl.ds(r, ROWS), cols]
        s = sinb[level, pl.ds(r, ROWS), cols]
        return re * c - im * s, re * s + im * c

    def source_turn(k):
        def body(r):
            for h in (0, 1):
                cols = slice(h * L, (h + 1) * L)
                re, im = turn(k, r, h, *y_value(0, r, h))
                slev[k + 1, pl.ds(r, ROWS), cols] = re
                slev[k + 1, pl.ds(L + r, ROWS), cols] = im
                put_x(r, h, re, im)

        rows_loop(body)

    def receiver_turn(k):
        level = jnp.maximum(DEPTH - 2 - k, 0)

        def body(r):
            for h in (0, 1):
                cols = slice(h * L, (h + 1) * L)
                re, im = y_value(1, r, h)
                rlev[DEPTH - 1 - k, pl.ds(r, ROWS), cols] = re
                rlev[DEPTH - 1 - k, pl.ds(L + r, ROWS), cols] = im
                put_x(r, h, *turn(level, r, h, re, im))

        rows_loop(body)

    def image(z):
        def body(r):
            img_o[z, pl.ds(r, ROWS), :] = (
                slev[z, pl.ds(r, ROWS), :] * rlev[z, pl.ds(r, ROWS), :]
                - slev[z, pl.ds(L + r, ROWS), :] * rlev[z, pl.ds(L + r, ROWS), :]
            )

        rows_loop(body)

    ins[0].wait()

    def first_source(r):
        for h in (0, 1):
            cols = slice(h * L, (h + 1) * L)
            put_x(r, h, slev[0, pl.ds(r, ROWS), cols], slev[0, pl.ds(L + r, ROWS), cols])

    rows_loop(first_source)
    carry(0, 0)
    ins[2].wait()
    for level in (DEPTH - 1, 0, DEPTH - 2):
        look_up(level)
    ins[1].wait()
    pl.semaphore_wait(barrier, nx * ny - 1)
    send(0, 0)
    local(0)

    def first_receiver(r):
        for h in (0, 1):
            cols = slice(h * L, (h + 1) * L)
            put_x(r, h, *turn(DEPTH - 1, r, h, rin[pl.ds(r, ROWS), cols], -rin[pl.ds(L + r, ROWS), cols]))

    rows_loop(first_receiver)
    start(1, 0)
    for level in range(1, DEPTH - 2):
        look_up(level)

    def step(k, state):
        pl.when(a < nx)(lambda: finish(0, k))
        source_turn(k)
        start(0, k + 1)
        pl.when(a < nx)(lambda: finish(1, k))
        receiver_turn(k)
        start(1, k + 1)

        return state

    lax.fori_loop(0, DEPTH - 1, step, 0)

    def last_source(r):
        for h in (0, 1):
            cols = slice(h * L, (h + 1) * L)
            re, im = turn(DEPTH - 1, r, h, *y_value(0, r, h))
            bot_o[pl.ds(r, ROWS), cols] = re
            bot_o[pl.ds(L + r, ROWS), cols] = im

    def last_receiver(r):
        for h in (0, 1):
            cols = slice(h * L, (h + 1) * L)
            re, im = y_value(1, r, h)
            top_o[pl.ds(r, ROWS), cols] = re
            top_o[pl.ds(L + r, ROWS), cols] = -im
            img_o[0, pl.ds(r, ROWS), cols] = slev[0, pl.ds(r, ROWS), cols] * re - slev[0, pl.ds(L + r, ROWS), cols] * im

    for z in range(DEPTH - 1, 0, -1):
        image(z)
    finish(0, DEPTH - 1)
    rows_loop(last_source)
    finish(1, DEPTH - 1)
    rows_loop(last_receiver)
    for f in (0, 1):
        for k in range(DEPTH):
            for kind in range(5):
                arrivals(kind, f, k).wait_send()


def write_out(image, bottom, top, image_o, bottom_o, top_o, sem):
    copies = [pltpu.make_async_copy(v, o, sem.at[i]) for i, (v, o) in enumerate(((image, image_o), (bottom, bottom_o), (top, top_o)))]
    for copy in copies:
        copy.start()
    for copy in copies:
        copy.wait()


def solution(mesh):
    nx, ny = mesh.shape["gx"], mesh.shape["gy"]

    def on_device(source_field, receiver_field, velocity_index, slowness, freq_index, root_modulus, root_angle):
        width = source_field.shape[3]
        any_spec = pl.BlockSpec(memory_space=pl.ANY)
        hbm = pl.BlockSpec(memory_space=pltpu.HBM)
        smem = pl.BlockSpec(memory_space=pltpu.SMEM)
        image, bottom, top = pl.pallas_call(
            functools.partial(kernel, nx, ny),
            out_shape=(
                jax.ShapeDtypeStruct((DEPTH, L, width), F32),
                jax.ShapeDtypeStruct((2 * L, width), F32),
                jax.ShapeDtypeStruct((2 * L, width), F32),
            ),
            in_specs=[hbm] * 4 + [smem] * 3,
            out_specs=(pl.BlockSpec(memory_space=pltpu.VMEM),) * 3,
            scratch_shapes=[
                pltpu.VMEM((DEPTH, 2 * L, width), F32),
                pltpu.VMEM((DEPTH, 2 * L, width), F32),
                pltpu.VMEM((2 * L, width), F32),
                pltpu.VMEM((DEPTH, L, width), jnp.int32),
                pltpu.VMEM((DEPTH, L, width), F32),
                pltpu.VMEM((DEPTH, L, width), F32),
                pltpu.VMEM((8, 128), F32),
                pltpu.VMEM((2, 2 * L, width), F32),
                pltpu.VMEM((2 * L, width), F32),
                pltpu.VMEM((6 * L, width), BF16),
                pltpu.VMEM((2 * L, 6 * L), BF16),
                pltpu.VMEM((4 * L, L), F32),
                pltpu.VMEM((2 * L, 6 * L), BF16),
                pltpu.VMEM((6 * L, 2 * L), BF16),
                pltpu.VMEM((2, 16, 4 * L), BF16),
                pltpu.VMEM((2, L, 3 * L), BF16),
                pltpu.VMEM((2, L, L), BF16),
                pltpu.VMEM((L, 4 * L), BF16),
                pltpu.VMEM((L, 4 * L), BF16),
                pltpu.VMEM((2, DEPTH, nx, 8, L), F32),
                pltpu.VMEM((2, DEPTH, ny, 8, L), F32),
                pltpu.VMEM((2, DEPTH, nx, 8, 128), F32),
                pltpu.VMEM((1, 64), F32),
                pltpu.SemaphoreType.DMA((4,)),
                pltpu.SemaphoreType.DMA((5, 2, DEPTH)),
                pltpu.SemaphoreType.DMA((5, 2, DEPTH)),
            ],
            compiler_params=pltpu.CompilerParams(collective_id=0, has_side_effects=True, vmem_limit_bytes=44 * 2**20),
        )(
            pltpu.with_memory_space_constraint(source_field.reshape(2 * L, width), pltpu.HBM),
            pltpu.with_memory_space_constraint(receiver_field.reshape(2 * L, width), pltpu.HBM),
            pltpu.with_memory_space_constraint(velocity_index, pltpu.HBM),
            pltpu.with_memory_space_constraint(slowness.reshape(1, -1), pltpu.HBM),
            freq_index,
            root_modulus,
            root_angle,
        )
        image, bottom, top = pl.pallas_call(
            write_out,
            out_shape=tuple(jax.ShapeDtypeStruct(v.shape, F32) for v in (image, bottom, top)),
            in_specs=[any_spec] * 3,
            out_specs=(any_spec,) * 3,
            scratch_shapes=[pltpu.SemaphoreType.DMA((3,))],
            compiler_params=pltpu.CompilerParams(vmem_limit_bytes=2**20),
        )(image, bottom, top)
        return image, bottom.reshape(source_field.shape), top.reshape(receiver_field.shape)

    wave = P(None, None, "gx", "gy")
    return jax.shard_map(
        on_device,
        mesh=mesh,
        in_specs=(wave, wave, P(None, "gx", "gy"), P(), P(), P(), P()),
        out_specs=(P(None, "gx", "gy"), wave, wave),
        check_vma=False,
    )
```

```python
import functools

import jax
import jax.numpy as jnp
from jax import lax
from jax.experimental import pallas as pl
from jax.experimental.pallas import tpu as pltpu
from jax.sharding import PartitionSpec as P

MESH = pl.DeviceIdType.MESH
F32 = jnp.float32
BF16 = jnp.bfloat16
L = 256
DEPTH = 4
PHASE_UNIT = 0.05
ROWS = 32


def cmul(a, b):
    return a[0] * b[0] - a[1] * b[1], a[0] * b[1] + a[1] * b[0]


def split(x):
    hi = x.astype(BF16)
    lo = (x - hi.astype(F32)).astype(BF16)
    return hi, lo


def mm(a, b):
    return jnp.dot(a, b, preferred_element_type=F32)


def mm_nt(a, b):
    return lax.dot_general(a, b, (((1,), (1,)), ((), ())), preferred_element_type=F32)


def iota(shape, dim):
    return lax.broadcasted_iota(jnp.int32, shape, dim)


def build_tables(nx, ny, a, b, modulus, angle, va_ref, vb_ref, vl_ref, kw_ref, qx_ref, qy_ref, qc_ref):
    one = jnp.full((8, 128), 1.0, F32)
    m = one * modulus
    th = one * angle
    d = 1.0 - m
    z = d / (2.0 - d)
    z2 = z * z
    logm = -2.0 * z * (1.0 + z2 * (1.0 / 3.0 + z2 * (0.2 + z2 * (1.0 / 7.0 + z2 * (1.0 / 9.0)))))
    ct, st = jnp.cos(th), jnp.sin(th)
    p = (m * ct, m * st)
    kappa = d * (1.0 + m)
    den = (kappa + 2.0 * m * m * st * st, -2.0 * m * m * st * ct)
    inv = 1.0 / (den[0] * den[0] + den[1] * den[1])
    rden = (den[0] * inv, -den[1] * inv)
    gamma = (kappa * kappa * rden[0], kappa * kappa * rden[1])
    beta = (-gamma[0], -gamma[1])
    alpha = cmul((2.0 * kappa * st * st, 2.0 * kappa * st * ct), rden)
    alpha_p = cmul(alpha, p)
    diag = (p[0] * p[0] - p[1] * p[1] + gamma[0], -2.0 * p[0] * p[1] + gamma[1])

    def sc(v):
        return v[0][0:1, 0:1], v[1][0:1, 0:1]

    row = iota((8, L), 0)
    col = iota((8, L), 1)
    expo = jnp.where(row == 0, col, jnp.where(row == 1, L - 1 - col, -col)).astype(F32)
    mag = jnp.exp(expo * logm[0:1, 0:1])
    turn = expo * th[0:1, 0:1]
    pw = (mag * jnp.cos(turn), mag * jnp.sin(turn))
    pw_t = tuple(jnp.concatenate([v] * 16, axis=0).T for v in pw)

    def prow(i):
        return pw[0][i : i + 1, :], pw[1][i : i + 1, :]

    def pcol(i):
        return pw_t[0][:, i : i + 1], pw_t[1][:, i : i + 1]

    h_r, g_r, n_r = prow(0), prow(1), prow(2)
    h_c, g_c, n_c = pcol(0), pcol(1), pcol(2)

    ii = iota((L, L), 0)
    jj = iota((L, L), 1)
    low = ii >= jj
    left = tuple(jnp.where(low, h_c[t], n_c[t]) for t in (0, 1))
    right = tuple(jnp.where(low, n_r[t], h_r[t]) for t in (0, 1))
    k_full = cmul(sc(alpha), cmul(left, right))
    dg = sc(diag)
    k_re = jnp.where(ii == jj, dg[0], k_full[0])
    k_im = jnp.where(ii == jj, dg[1], k_full[1])
    for part, sign_ab in ((k_re, None), (k_im, 1)):
        hi, lo = split(part)
        for which, piece in ((0, hi), (1, lo)):
            if sign_ab is None:
                spots_a = (((0, 0), piece), ((L, L), piece))
                spots_b = spots_a
            else:
                spots_a = (((0, L), -piece), ((L, 0), piece))
                spots_b = (((0, L), piece), ((L, 0), -piece))
            for (r0, c0), val in spots_a:
                if which == 0:
                    va_ref[r0 : r0 + L, c0 : c0 + L] = val
                    va_ref[r0 : r0 + L, 2 * L + c0 : 3 * L + c0] = val
                else:
                    va_ref[r0 : r0 + L, 4 * L + c0 : 5 * L + c0] = val
            for (r0, c0), val in spots_b:
                if which == 0:
                    vb_ref[r0 : r0 + L, c0 : c0 + L] = val
                    vb_ref[2 * L + r0 : 3 * L + r0, c0 : c0 + L] = val
                else:
                    vb_ref[4 * L + r0 : 5 * L + r0, c0 : c0 + L] = val

    r8 = iota((8, L), 0)
    end8 = (r8 & 1) == 1
    v_re = jnp.where(end8, h_r[0], g_r[0])
    v_im = jnp.where(end8, h_r[1], g_r[1])
    imag8 = ((r8 >> 1) & 1) == 1
    v_parts = (jnp.where(imag8, v_im, v_re), jnp.where(imag8, v_re, -v_im))
    for h in (0, 1):
        mine = (r8 >> 2) == h
        for part in (0, 1):
            val = jnp.where(mine, v_parts[part], 0.0)
            hi = val.astype(BF16).astype(F32)
            lo = val - hi
            vl_ref[h, :, part * L : (part + 1) * L] = jnp.concatenate([hi, lo], axis=0).astype(BF16)
            vl_ref[h, :, (2 + part) * L : (3 + part) * L] = jnp.concatenate([hi, jnp.zeros_like(hi)], axis=0).astype(BF16)

    lane = iota((L, 128), 1)
    end_l = ((lane >> 1) & 1) == 1
    imag_l = (lane & 1) == 1
    c_re = jnp.where(end_l, h_c[0], g_c[0])
    c_im = jnp.where(end_l, h_c[1], g_c[1])
    for c0, val in (
        (0, k_re), (L, k_im),
        (2 * L, jnp.where(imag_l, c_im, c_re)),
        (2 * L + 128, jnp.where(imag_l, c_re, -c_im)),
    ):
        hi, lo = split(val)
        kw_ref[0, :, c0 : c0 + val.shape[1]] = hi
        kw_ref[1, :, c0 : c0 + val.shape[1]] = lo

    rr = iota((16, 128), 0)
    kk = iota((16, 128), 1)
    is_x = rr < 2
    is_c = rr >= 6
    target = jnp.where(is_x, a, 2 * b + jnp.where(is_c, (rr - 6) >> 1, (rr - 2) >> 1))
    kk = kk & 63
    source = kk >> 2
    count = jnp.where(is_x, nx, 2 * ny)
    is_s = (rr & 1) == 0
    is_e = jnp.where(is_c, (kk >> 1) & 1, kk & 1) == 1
    is_i = jnp.where(is_c, kk & 1, (kk >> 1) & 1) == 1
    steps = jnp.where(is_s, target - 1 - source, jnp.where(is_e, source - target - 1, 2 * count - 2 - target - source))
    valid = (steps >= 0) & (source < count) & jnp.logical_not(is_s & is_e)
    use_beta = jnp.logical_not(is_s) & jnp.logical_not(is_e)
    n = jnp.maximum(steps, 0).astype(F32)
    th_l = th * float(L)
    wraps = jnp.floor(th_l * 0.15915494309189535 + 0.5)
    th_l = (th_l - wraps * 6.28125) - wraps * 0.0019353071795864769
    mag = jnp.exp(n * (logm[0:1, :] * float(L)))
    om = (mag * jnp.cos(n * th_l[0:1, :]), mag * jnp.sin(n * th_l[0:1, :]))
    coef = tuple(jnp.where(use_beta, beta[t][0:1, :], alpha_p[t][0:1, :]) for t in (0, 1))
    om = cmul(om, coef)
    om = (jnp.where(is_i, -om[1], om[0]), jnp.where(is_i, om[0], om[1]))
    om = tuple(jnp.where(valid, v, 0.0) for v in om)
    om_t = tuple(jnp.concatenate([v] * 8, axis=0).T for v in om)

    first_half = iota((L, 128), 1) < 64
    q1 = cmul(h_c, (om[0][0:1, :], om[1][0:1, :]))
    q2 = cmul(g_c, (om[0][1:2, :], om[1][1:2, :]))
    for part in (0, 1):
        val = q1[part] + q2[part]
        hi = val.astype(BF16).astype(F32)
        qx_ref[part, :, 0:128] = hi.astype(BF16)
        qx_ref[part, :, 128:256] = jnp.where(first_half, val - hi, 0.0).astype(BF16)
    for first, ref in ((2, qy_ref), (6, qc_ref)):
        for h in (0, 1):
            w_s = tuple(om_t[t][:64, first + 2 * h : first + 2 * h + 1] for t in (0, 1))
            w_t = tuple(om_t[t][:64, first + 2 * h + 1 : first + 2 * h + 2] for t in (0, 1))
            q1 = cmul(w_s, h_r)
            q2 = cmul(w_t, g_r)
            for part in (0, 1):
                hi, lo = split(q1[part] + q2[part])
                cols = slice((2 * h + part) * L, (2 * h + part + 1) * L)
                ref[0:64, cols] = hi
                ref[64:128, cols] = hi
                ref[128:192, cols] = lo
        ref[192:256, :] = jnp.zeros((64, 4 * L), BF16)


def kernel(
    nx, ny,
    src, rec, vidx, slow_h, freq, mod, ang,
    img_o, bot_o, top_o,
    slev, rlev, rin, vin, cosb, sinb, tab, u_ref, w_ref, hl, hly, xy, yo,
    va, vb, vl, kw, qx, qy, qc, gxb, gyb, ccb,
    slow, in_sem, send_sem, recv_sem,
):
    a = lax.axis_index("gx")
    b = lax.axis_index("gy")
    ins = [
        pltpu.make_async_copy(src, slev.at[0], in_sem.at[0]),
        pltpu.make_async_copy(rec, rin, in_sem.at[1]),
        pltpu.make_async_copy(vidx, vin, in_sem.at[2]),
        pltpu.make_async_copy(slow_h, slow, in_sem.at[3]),
    ]
    for copy in ins:
        copy.start()

    def ring(i):
        return min(i, 4 - i)

    if nx == 16:
        ax, ay = a // 4, a % 4
        x_peers = [(ring(i) + ring(j), lax.rem(ax + i, 4) * 4 + lax.rem(ay + j, 4)) for i in range(4) for j in range(4) if i or j]
    else:
        x_peers = [(0, lax.rem(a + o, nx)) for o in range(1, nx)]
    y_peers = [(min(o // 2, (ny - o) // 2), lax.rem(b + o, ny)) for o in range(1, ny)]
    peers = [(d, 0, {"gx": p}) for d, p in x_peers] + [(d, 1, {"gy": p}) for d, p in y_peers]
    peers += [(d, 3, {"gx": p}) for d, p in x_peers] + [(d, 4, {"gy": p}) for d, p in y_peers]
    peers += [(d + e, 2, {"gx": p, "gy": q}) for d, p in x_peers for e, q in y_peers]
    peers.sort(key=lambda t: (-t[0], t[1]))

    barrier = pltpu.get_barrier_semaphore()
    for _, kind, peer in peers:
        if kind < 3:
            pl.semaphore_signal(barrier, inc=1, device_id=peer, device_id_type=MESH)

    if ny < 8:
        ccb[...] = jnp.zeros_like(ccb)
    build_tables(nx, ny, a, b, mod[0], ang[0], va, vb, vl, kw, qx, qy, qc)
    ins[3].wait()
    tab[...] = jnp.zeros((8, 128), F32)
    tab[0:1, 0:64] = slow[...]
    rate = jnp.full((8, 128), 1.0, F32) * freq[0].astype(F32) * PHASE_UNIT
    arg = rate * tab[...]
    cos_tab = jnp.broadcast_to(jnp.cos(arg)[0:1, :], (ROWS, 128))
    sin_tab = jnp.broadcast_to(jnp.sin(arg)[0:1, :], (ROWS, 128))

    def rows_loop(body):
        def go(i, carry):
            body(pl.multiple_of(i * ROWS, ROWS))
            return carry

        lax.fori_loop(0, L // ROWS, go, 0)

    def look_up(level):
        def body(r):
            for c in range(4):
                idx = vin[level, pl.ds(r, ROWS), c * 128 : (c + 1) * 128]
                cosb[level, pl.ds(r, ROWS), c * 128 : (c + 1) * 128] = jnp.take_along_axis(cos_tab, idx, axis=1, mode="promise_in_bounds")
                sinb[level, pl.ds(r, ROWS), c * 128 : (c + 1) * 128] = jnp.take_along_axis(sin_tab, idx, axis=1, mode="promise_in_bounds")

        rows_loop(body)

    def put_x(r, h, re, im):
        cols = slice(h * L, (h + 1) * L)
        for part, val in ((0, re), (1, im)):
            hi, lo = split(val)
            hl[pl.ds(part * L + r, ROWS), cols] = hi
            hl[pl.ds((2 + part) * L + r, ROWS), cols] = lo
            hl[pl.ds((4 + part) * L + r, ROWS), cols] = hi

    def slot(kind, f, k):
        if kind == 0:
            return gxb.at[f, k, a]
        if kind == 1:
            return gyb.at[f, k, b]
        return ccb.at[f, k, a, pl.ds(b, 1)]

    def arrivals(kind, f, k):
        block = (
            gxb.at[f, k, pl.ds(0, nx - 1)],
            gyb.at[f, k, pl.ds(0, ny - 1)],
            ccb.at[f, k, pl.ds(0, nx - 1), pl.ds(0, ny - 1)],
            ccb.at[f, k, pl.ds(0, nx - 1), pl.ds(0, 1)],
            ccb.at[f, k, 0, pl.ds(0, ny - 1)],
        )[kind]
        return pltpu.make_async_remote_copy(block, block, send_sem.at[kind, f, k], recv_sem.at[kind, f, k], device_id={"gx": a}, device_id_type=MESH)

    real8 = ((iota((8, L), 0) >> 1) & 1) == 0
    lane8, row8 = iota((8, 128), 1), iota((8, 128), 0)
    corner_mask = (((row8 >> 1) & 1) == 0) & ((lane8 >> 6) == (row8 & 1)) & (((lane8 >> 2) & 1) == (row8 >> 2)) & (((lane8 >> 3) & 7) == b)

    def times_i(q):
        return jnp.where(real8, -pltpu.roll(q, 6, 0), pltpu.roll(q, 2, 0))

    def local(f):
        w_ref[...] = mm(va[...], hl[...])

        def body(r):
            for h in (0, 1):
                for part in (0, 1):
                    hi, lo = split(w_ref[pl.ds(part * L + r, ROWS), h * L : (h + 1) * L])
                    hly[pl.ds(h * L + r, ROWS), part * L : (part + 1) * L] = hi
                    hly[pl.ds(h * L + r, ROWS), (2 + part) * L : (3 + part) * L] = lo
                    hly[pl.ds(h * L + r, ROWS), (4 + part) * L : (5 + part) * L] = hi

        rows_loop(body)
        u_ref[f] = mm(hly[...], vb[...])

    def carry(f, k):
        acc_x = acc_y = jnp.zeros((16, L), F32)
        for h in (0, 1):
            cols = slice(h * L, (h + 1) * L)
            acc_x = acc_x + mm(vl[h], hl[0 : 4 * L, cols])
            for i in range(4):
                acc_y = acc_y + mm_nt(vl[h, :, i * L : (i + 1) * L], hl[i * L : (i + 1) * L, cols])
        carries = jnp.concatenate([acc_x[0:8] + acc_x[8:16], acc_y[0:8] + acc_y[8:16]], axis=0)
        hi = carries.astype(BF16).astype(F32)
        both = jnp.concatenate([hi, carries - hi], axis=0).astype(BF16)
        out = mm(both, kw[0])
        out = out[0:16] + out[16:32] + mm(both[0:16], kw[1])
        gxb[f, k, a] = out[0:8, 0:L] + times_i(out[0:8, L : 2 * L])
        gyb[f, k, b] = out[8:16, 0:L] + times_i(out[8:16, L : 2 * L])
        corner = out[0:8, 2 * L : 2 * L + 128] + pltpu.roll(out[0:8, 2 * L + 128 : 3 * L], 6, 0)
        ccb[f, k, a, pl.ds(b, 1)] = jnp.sum(jnp.where(corner_mask, corner, 0.0), axis=0, keepdims=True)
    def send(f, k):
        for _, kind, peer in peers:
            here = slot(kind, f, k)
            pltpu.make_async_remote_copy(here, here, send_sem.at[kind, f, k], recv_sem.at[kind, f, k], device_id=peer, device_id_type=MESH).start()

    def start(f, k):
        carry(f, k)
        send(f, k)
        pl.when(a < nx)(lambda: local(f))

    def finish(f, k):
        for kind in (1, 0):
            arrivals(kind, f, k).wait_recv()
        gy = gyb[f, k].reshape(8 * ny, L)
        hi = gy.astype(BF16).astype(F32)
        fill = [jnp.zeros((64 - 8 * ny, L), F32)] if 8 * ny < 64 else []
        gy3 = jnp.concatenate([hi] + fill + [gy - hi] + fill + [hi] + fill + [jnp.zeros((64, L), F32)], axis=0).T.astype(BF16)
        yo[...] = mm(gy3, qy[...])
        for kind in (2, 3, 4):
            arrivals(kind, f, k).wait_recv()
        pairs = nx // 2
        m = jnp.sum(ccb[f, k], axis=1, keepdims=True).reshape(pairs, 2, 1, 128)
        shape = (pairs, 8, 128)
        m = jnp.where(iota(shape, 1) < 4, jnp.broadcast_to(m[:, 0], shape), jnp.broadcast_to(m[:, 1], shape)).reshape(4 * nx, 128)
        left = iota((4 * nx, 128), 1) < 64
        row = iota((4 * nx, 128), 0)
        m = jnp.where((row & 1) == 1, pltpu.roll(m, 64, 1), m)
        hi = m.astype(BF16).astype(F32)
        m = jnp.concatenate([jnp.where(left, hi, pltpu.roll(m - hi, 64, 1)), jnp.where(left, hi, 0.0)], axis=1).astype(BF16)
        corr = mm(m, qc[...])
        real = ((iota((4 * nx, L), 0) >> 1) & 1) == 0
        g = gxb[f, k].reshape(pairs, 2, 8, L)
        even, odd = g[:, 0], g[:, 1]
        top = iota((pairs, 8, L), 1) < 4
        g = (jnp.where(top, even, pltpu.roll(odd, 4, 1)), jnp.where(top, pltpu.roll(even, 4, 1), odd))
        gx3 = []
        for h in (0, 1):
            val = g[h].reshape(4 * nx, L) + jnp.where(real, corr[:, 2 * h * L : (2 * h + 1) * L], corr[:, (2 * h + 1) * L : (2 * h + 2) * L])
            hi, lo = split(val)
            pad = jnp.zeros((64 - 4 * nx, L), BF16)
            fill = [pad] if 4 * nx < 64 else []
            gx3.append(jnp.concatenate([hi] + fill + [lo] + fill + [hi] + fill + [jnp.zeros((64, L), BF16)], axis=0))
        for h in (0, 1):
            xy[2 * h * L : 2 * (h + 1) * L, :] = mm(qx[...].reshape(2 * L, L), gx3[h])

    def y_value(f, r, h):
        re = u_ref[f, pl.ds(h * L + r, ROWS), 0:L] + (xy[pl.ds(2 * h * L + r, ROWS), :] + yo[pl.ds(r, ROWS), 2 * h * L : (2 * h + 1) * L])
        im = u_ref[f, pl.ds(h * L + r, ROWS), L : 2 * L] + (xy[pl.ds((2 * h + 1) * L + r, ROWS), :] + yo[pl.ds(r, ROWS), (2 * h + 1) * L : (2 * h + 2) * L])
        return re, im

    def turn(level, r, h, re, im):
        cols = slice(h * L, (h + 1) * L)
        c = cosb[level, pl.ds(r, ROWS), cols]
        s = sinb[level, pl.ds(r, ROWS), cols]
        return re * c - im * s, re * s + im * c

    def source_turn(k):
        def body(r):
            for h in (0, 1):
                cols = slice(h * L, (h + 1) * L)
                re, im = turn(k, r, h, *y_value(0, r, h))
                slev[k + 1, pl.ds(r, ROWS), cols] = re
                slev[k + 1, pl.ds(L + r, ROWS), cols] = im
                put_x(r, h, re, im)

        rows_loop(body)

    def receiver_turn(k):
        level = jnp.maximum(DEPTH - 2 - k, 0)

        def body(r):
            for h in (0, 1):
                cols = slice(h * L, (h + 1) * L)
                re, im = y_value(1, r, h)
                rlev[DEPTH - 1 - k, pl.ds(r, ROWS), cols] = re
                rlev[DEPTH - 1 - k, pl.ds(L + r, ROWS), cols] = im
                put_x(r, h, *turn(level, r, h, re, im))

        rows_loop(body)

    def image(z):
        def body(r):
            img_o[z, pl.ds(r, ROWS), :] = (
                slev[z, pl.ds(r, ROWS), :] * rlev[z, pl.ds(r, ROWS), :]
                - slev[z, pl.ds(L + r, ROWS), :] * rlev[z, pl.ds(L + r, ROWS), :]
            )

        rows_loop(body)

    ins[0].wait()

    def first_source(r):
        for h in (0, 1):
            cols = slice(h * L, (h + 1) * L)
            put_x(r, h, slev[0, pl.ds(r, ROWS), cols], slev[0, pl.ds(L + r, ROWS), cols])

    rows_loop(first_source)
    carry(0, 0)
    ins[2].wait()
    for level in (DEPTH - 1, 0, DEPTH - 2):
        look_up(level)
    ins[1].wait()
    pl.semaphore_wait(barrier, nx * ny - 1)
    send(0, 0)
    local(0)

    def first_receiver(r):
        for h in (0, 1):
            cols = slice(h * L, (h + 1) * L)
            put_x(r, h, *turn(DEPTH - 1, r, h, rin[pl.ds(r, ROWS), cols], -rin[pl.ds(L + r, ROWS), cols]))

    rows_loop(first_receiver)
    start(1, 0)
    for level in range(1, DEPTH - 2):
        look_up(level)

    def step(k, state):
        pl.when(a < nx)(lambda: finish(0, k))
        source_turn(k)
        start(0, k + 1)
        pl.when(a < nx)(lambda: finish(1, k))
        receiver_turn(k)
        start(1, k + 1)

        return state

    lax.fori_loop(0, DEPTH - 1, step, 0)

    def last_source(r):
        for h in (0, 1):
            cols = slice(h * L, (h + 1) * L)
            re, im = turn(DEPTH - 1, r, h, *y_value(0, r, h))
            bot_o[pl.ds(r, ROWS), cols] = re
            bot_o[pl.ds(L + r, ROWS), cols] = im

    def last_receiver(r):
        for h in (0, 1):
            cols = slice(h * L, (h + 1) * L)
            re, im = y_value(1, r, h)
            top_o[pl.ds(r, ROWS), cols] = re
            top_o[pl.ds(L + r, ROWS), cols] = -im
            img_o[0, pl.ds(r, ROWS), cols] = slev[0, pl.ds(r, ROWS), cols] * re - slev[0, pl.ds(L + r, ROWS), cols] * im

    for z in range(DEPTH - 1, 0, -1):
        image(z)
    finish(0, DEPTH - 1)
    rows_loop(last_source)
    finish(1, DEPTH - 1)
    rows_loop(last_receiver)
    for f in (0, 1):
        for k in range(DEPTH):
            for kind in range(5):
                arrivals(kind, f, k).wait_send()


def write_out(image, bottom, top, image_o, bottom_o, top_o, sem):
    copies = [pltpu.make_async_copy(v, o, sem.at[i]) for i, (v, o) in enumerate(((image, image_o), (bottom, bottom_o), (top, top_o)))]
    for copy in copies:
        copy.start()
    for copy in copies:
        copy.wait()


def solution(mesh):
    nx, ny = mesh.shape["gx"], mesh.shape["gy"]

    def on_device(source_field, receiver_field, velocity_index, slowness, freq_index, root_modulus, root_angle):
        width = source_field.shape[3]
        any_spec = pl.BlockSpec(memory_space=pl.ANY)
        hbm = pl.BlockSpec(memory_space=pltpu.HBM)
        smem = pl.BlockSpec(memory_space=pltpu.SMEM)
        image, bottom, top = pl.pallas_call(
            functools.partial(kernel, nx, ny),
            out_shape=(
                jax.ShapeDtypeStruct((DEPTH, L, width), F32),
                jax.ShapeDtypeStruct((2 * L, width), F32),
                jax.ShapeDtypeStruct((2 * L, width), F32),
            ),
            in_specs=[hbm] * 4 + [smem] * 3,
            out_specs=(pl.BlockSpec(memory_space=pltpu.VMEM),) * 3,
            scratch_shapes=[
                pltpu.VMEM((DEPTH, 2 * L, width), F32),
                pltpu.VMEM((DEPTH, 2 * L, width), F32),
                pltpu.VMEM((2 * L, width), F32),
                pltpu.VMEM((DEPTH, L, width), jnp.int32),
                pltpu.VMEM((DEPTH, L, width), F32),
                pltpu.VMEM((DEPTH, L, width), F32),
                pltpu.VMEM((8, 128), F32),
                pltpu.VMEM((2, 2 * L, width), F32),
                pltpu.VMEM((2 * L, width), F32),
                pltpu.VMEM((6 * L, width), BF16),
                pltpu.VMEM((2 * L, 6 * L), BF16),
                pltpu.VMEM((4 * L, L), F32),
                pltpu.VMEM((L, 4 * L), F32),
                pltpu.VMEM((2 * L, 6 * L), BF16),
                pltpu.VMEM((6 * L, 2 * L), BF16),
                pltpu.VMEM((2, 16, 4 * L), BF16),
                pltpu.VMEM((2, L, 3 * L), BF16),
                pltpu.VMEM((2, L, L), BF16),
                pltpu.VMEM((L, 4 * L), BF16),
                pltpu.VMEM((L, 4 * L), BF16),
                pltpu.VMEM((2, DEPTH, nx, 8, L), F32),
                pltpu.VMEM((2, DEPTH, ny, 8, L), F32),
                pltpu.VMEM((2, DEPTH, nx, 8, 128), F32),
                pltpu.VMEM((1, 64), F32),
                pltpu.SemaphoreType.DMA((4,)),
                pltpu.SemaphoreType.DMA((5, 2, DEPTH)),
                pltpu.SemaphoreType.DMA((5, 2, DEPTH)),
            ],
            compiler_params=pltpu.CompilerParams(collective_id=0, has_side_effects=True, vmem_limit_bytes=44 * 2**20),
        )(
            pltpu.with_memory_space_constraint(source_field.reshape(2 * L, width), pltpu.HBM),
            pltpu.with_memory_space_constraint(receiver_field.reshape(2 * L, width), pltpu.HBM),
            pltpu.with_memory_space_constraint(velocity_index, pltpu.HBM),
            pltpu.with_memory_space_constraint(slowness.reshape(1, -1), pltpu.HBM),
            freq_index,
            root_modulus,
            root_angle,
        )
        image, bottom, top = pl.pallas_call(
            write_out,
            out_shape=tuple(jax.ShapeDtypeStruct(v.shape, F32) for v in (image, bottom, top)),
            in_specs=[any_spec] * 3,
            out_specs=(any_spec,) * 3,
            scratch_shapes=[pltpu.SemaphoreType.DMA((3,))],
            compiler_params=pltpu.CompilerParams(vmem_limit_bytes=2**20),
        )(image, bottom, top)
        return image, bottom.reshape(source_field.shape), top.reshape(receiver_field.shape)

    wave = P(None, None, "gx", "gy")
    return jax.shard_map(
        on_device,
        mesh=mesh,
        in_specs=(wave, wave, P(None, "gx", "gy"), P(), P(), P(), P()),
        out_specs=(P(None, "gx", "gy"), wave, wave),
        check_vma=False,
    )
```

```python
import functools

import jax
import jax.numpy as jnp
from jax import lax
from jax.experimental import pallas as pl
from jax.experimental.pallas import tpu as pltpu
from jax.sharding import PartitionSpec as P

MESH = pl.DeviceIdType.MESH
F32 = jnp.float32
BF16 = jnp.bfloat16
L = 256
DEPTH = 4
PHASE_UNIT = 0.05
ROWS = 32


def cmul(a, b):
    return a[0] * b[0] - a[1] * b[1], a[0] * b[1] + a[1] * b[0]


def split(x):
    hi = x.astype(BF16)
    lo = (x - hi.astype(F32)).astype(BF16)
    return hi, lo


def mm(a, b):
    return jnp.dot(a, b, preferred_element_type=F32)


def mm_nt(a, b):
    return lax.dot_general(a, b, (((1,), (1,)), ((), ())), preferred_element_type=F32)


def iota(shape, dim):
    return lax.broadcasted_iota(jnp.int32, shape, dim)


def build_tables(nx, ny, a, b, modulus, angle, va_ref, vb_ref, vl_ref, kw_ref, qx_ref, qy_ref, qc_ref):
    one = jnp.full((8, 128), 1.0, F32)
    m = one * modulus
    th = one * angle
    d = 1.0 - m
    z = d / (2.0 - d)
    z2 = z * z
    logm = -2.0 * z * (1.0 + z2 * (1.0 / 3.0 + z2 * (0.2 + z2 * (1.0 / 7.0 + z2 * (1.0 / 9.0)))))
    ct, st = jnp.cos(th), jnp.sin(th)
    p = (m * ct, m * st)
    kappa = d * (1.0 + m)
    den = (kappa + 2.0 * m * m * st * st, -2.0 * m * m * st * ct)
    inv = 1.0 / (den[0] * den[0] + den[1] * den[1])
    rden = (den[0] * inv, -den[1] * inv)
    gamma = (kappa * kappa * rden[0], kappa * kappa * rden[1])
    beta = (-gamma[0], -gamma[1])
    alpha = cmul((2.0 * kappa * st * st, 2.0 * kappa * st * ct), rden)
    alpha_p = cmul(alpha, p)
    diag = (p[0] * p[0] - p[1] * p[1] + gamma[0], -2.0 * p[0] * p[1] + gamma[1])

    def sc(v):
        return v[0][0:1, 0:1], v[1][0:1, 0:1]

    row = iota((8, L), 0)
    col = iota((8, L), 1)
    expo = jnp.where(row == 0, col, jnp.where(row == 1, L - 1 - col, -col)).astype(F32)
    mag = jnp.exp(expo * logm[0:1, 0:1])
    turn = expo * th[0:1, 0:1]
    pw = (mag * jnp.cos(turn), mag * jnp.sin(turn))
    pw_t = tuple(jnp.concatenate([v] * 16, axis=0).T for v in pw)

    def prow(i):
        return pw[0][i : i + 1, :], pw[1][i : i + 1, :]

    def pcol(i):
        return pw_t[0][:, i : i + 1], pw_t[1][:, i : i + 1]

    h_r, g_r, n_r = prow(0), prow(1), prow(2)
    h_c, g_c, n_c = pcol(0), pcol(1), pcol(2)

    ii = iota((L, L), 0)
    jj = iota((L, L), 1)
    low = ii >= jj
    left = tuple(jnp.where(low, h_c[t], n_c[t]) for t in (0, 1))
    right = tuple(jnp.where(low, n_r[t], h_r[t]) for t in (0, 1))
    k_full = cmul(sc(alpha), cmul(left, right))
    dg = sc(diag)
    k_re = jnp.where(ii == jj, dg[0], k_full[0])
    k_im = jnp.where(ii == jj, dg[1], k_full[1])
    for part, sign_ab in ((k_re, None), (k_im, 1)):
        hi, lo = split(part)
        for which, piece in ((0, hi), (1, lo)):
            if sign_ab is None:
                spots_a = (((0, 0), piece), ((L, L), piece))
                spots_b = spots_a
            else:
                spots_a = (((0, L), -piece), ((L, 0), piece))
                spots_b = (((0, L), piece), ((L, 0), -piece))
            for (r0, c0), val in spots_a:
                if which == 0:
                    va_ref[r0 : r0 + L, c0 : c0 + L] = val
                    va_ref[r0 : r0 + L, 2 * L + c0 : 3 * L + c0] = val
                else:
                    va_ref[r0 : r0 + L, 4 * L + c0 : 5 * L + c0] = val
            for (r0, c0), val in spots_b:
                if which == 0:
                    vb_ref[r0 : r0 + L, c0 : c0 + L] = val
                    vb_ref[2 * L + r0 : 3 * L + r0, c0 : c0 + L] = val
                else:
                    vb_ref[4 * L + r0 : 5 * L + r0, c0 : c0 + L] = val

    r8 = iota((8, L), 0)
    end8 = (r8 & 1) == 1
    v_re = jnp.where(end8, h_r[0], g_r[0])
    v_im = jnp.where(end8, h_r[1], g_r[1])
    imag8 = ((r8 >> 1) & 1) == 1
    v_parts = (jnp.where(imag8, v_im, v_re), jnp.where(imag8, v_re, -v_im))
    for h in (0, 1):
        mine = (r8 >> 2) == h
        for part in (0, 1):
            val = jnp.where(mine, v_parts[part], 0.0)
            hi = val.astype(BF16).astype(F32)
            lo = val - hi
            vl_ref[h, :, part * L : (part + 1) * L] = jnp.concatenate([hi, lo], axis=0).astype(BF16)
            vl_ref[h, :, (2 + part) * L : (3 + part) * L] = jnp.concatenate([hi, jnp.zeros_like(hi)], axis=0).astype(BF16)

    lane = iota((L, 128), 1)
    end_l = ((lane >> 1) & 1) == 1
    imag_l = (lane & 1) == 1
    c_re = jnp.where(end_l, h_c[0], g_c[0])
    c_im = jnp.where(end_l, h_c[1], g_c[1])
    for c0, val in (
        (0, k_re), (L, k_im),
        (2 * L, jnp.where(imag_l, c_im, c_re)),
        (2 * L + 128, jnp.where(imag_l, c_re, -c_im)),
    ):
        hi, lo = split(val)
        kw_ref[0, :, c0 : c0 + val.shape[1]] = hi
        kw_ref[1, :, c0 : c0 + val.shape[1]] = lo

    rr = iota((16, 128), 0)
    kk = iota((16, 128), 1)
    is_x = rr < 2
    is_c = rr >= 6
    target = jnp.where(is_x, a, 2 * b + jnp.where(is_c, (rr - 6) >> 1, (rr - 2) >> 1))
    kk = kk & 63
    source = kk >> 2
    count = jnp.where(is_x, nx, 2 * ny)
    is_s = (rr & 1) == 0
    is_e = jnp.where(is_c, (kk >> 1) & 1, kk & 1) == 1
    is_i = jnp.where(is_c, kk & 1, (kk >> 1) & 1) == 1
    steps = jnp.where(is_s, target - 1 - source, jnp.where(is_e, source - target - 1, 2 * count - 2 - target - source))
    valid = (steps >= 0) & (source < count) & jnp.logical_not(is_s & is_e)
    use_beta = jnp.logical_not(is_s) & jnp.logical_not(is_e)
    n = jnp.maximum(steps, 0).astype(F32)
    th_l = th * float(L)
    wraps = jnp.floor(th_l * 0.15915494309189535 + 0.5)
    th_l = (th_l - wraps * 6.28125) - wraps * 0.0019353071795864769
    mag = jnp.exp(n * (logm[0:1, :] * float(L)))
    om = (mag * jnp.cos(n * th_l[0:1, :]), mag * jnp.sin(n * th_l[0:1, :]))
    coef = tuple(jnp.where(use_beta, beta[t][0:1, :], alpha_p[t][0:1, :]) for t in (0, 1))
    om = cmul(om, coef)
    om = (jnp.where(is_i, -om[1], om[0]), jnp.where(is_i, om[0], om[1]))
    om = tuple(jnp.where(valid, v, 0.0) for v in om)
    om_t = tuple(jnp.concatenate([v] * 8, axis=0).T for v in om)

    first_half = iota((L, 128), 1) < 64
    q1 = cmul(h_c, (om[0][0:1, :], om[1][0:1, :]))
    q2 = cmul(g_c, (om[0][1:2, :], om[1][1:2, :]))
    for part in (0, 1):
        val = q1[part] + q2[part]
        hi = val.astype(BF16).astype(F32)
        qx_ref[part, :, 0:128] = hi.astype(BF16)
        qx_ref[part, :, 128:256] = jnp.where(first_half, val - hi, 0.0).astype(BF16)
    for first, ref in ((2, qy_ref), (6, qc_ref)):
        for h in (0, 1):
            w_s = tuple(om_t[t][:64, first + 2 * h : first + 2 * h + 1] for t in (0, 1))
            w_t = tuple(om_t[t][:64, first + 2 * h + 1 : first + 2 * h + 2] for t in (0, 1))
            q1 = cmul(w_s, h_r)
            q2 = cmul(w_t, g_r)
            for part in (0, 1):
                hi, lo = split(q1[part] + q2[part])
                cols = slice((2 * h + part) * L, (2 * h + part + 1) * L)
                ref[0:64, cols] = hi
                ref[64:128, cols] = hi
                ref[128:192, cols] = lo
        ref[192:256, :] = jnp.zeros((64, 4 * L), BF16)


def kernel(
    nx, ny,
    src, rec, vidx, slow_h, freq, mod, ang,
    img_o, bot_o, top_o,
    slev, rlev, rin, vin, cosb, sinb, tab, u_ref, w_ref, hl, hly, xy,
    va, vb, vl, kw, qx, qy, qc, gxb, gyb, ccb,
    slow, in_sem, send_sem, recv_sem,
):
    a = lax.axis_index("gx")
    b = lax.axis_index("gy")
    ins = [
        pltpu.make_async_copy(src, slev.at[0], in_sem.at[0]),
        pltpu.make_async_copy(rec, rin, in_sem.at[1]),
        pltpu.make_async_copy(vidx, vin, in_sem.at[2]),
        pltpu.make_async_copy(slow_h, slow, in_sem.at[3]),
    ]
    for copy in ins:
        copy.start()

    def ring(i):
        return min(i, 4 - i)

    if nx == 16:
        ax, ay = a // 4, a % 4
        x_peers = [(ring(i) + ring(j), lax.rem(ax + i, 4) * 4 + lax.rem(ay + j, 4)) for i in range(4) for j in range(4) if i or j]
    else:
        x_peers = [(0, lax.rem(a + o, nx)) for o in range(1, nx)]
    y_peers = [(min(o // 2, (ny - o) // 2), lax.rem(b + o, ny)) for o in range(1, ny)]
    peers = [(d, 0, {"gx": p}) for d, p in x_peers] + [(d, 1, {"gy": p}) for d, p in y_peers]
    peers += [(d, 3, {"gx": p}) for d, p in x_peers] + [(d, 4, {"gy": p}) for d, p in y_peers]
    peers += [(d + e, 2, {"gx": p, "gy": q}) for d, p in x_peers for e, q in y_peers]
    peers.sort(key=lambda t: (-t[0], t[1]))

    barrier = pltpu.get_barrier_semaphore()
    for _, kind, peer in peers:
        if kind < 3:
            pl.semaphore_signal(barrier, inc=1, device_id=peer, device_id_type=MESH)

    if ny < 8:
        ccb[...] = jnp.zeros_like(ccb)
    build_tables(nx, ny, a, b, mod[0], ang[0], va, vb, vl, kw, qx, qy, qc)
    ins[3].wait()
    tab[...] = jnp.zeros((8, 128), F32)
    tab[0:1, 0:64] = slow[...]
    rate = jnp.full((8, 128), 1.0, F32) * freq[0].astype(F32) * PHASE_UNIT
    arg = rate * tab[...]
    cos_tab = jnp.broadcast_to(jnp.cos(arg)[0:1, :], (ROWS, 128))
    sin_tab = jnp.broadcast_to(jnp.sin(arg)[0:1, :], (ROWS, 128))

    def rows_loop(body):
        def go(i, carry):
            body(pl.multiple_of(i * ROWS, ROWS))
            return carry

        lax.fori_loop(0, L // ROWS, go, 0)

    def look_up(level):
        def body(r):
            for c in range(4):
                idx = vin[level, pl.ds(r, ROWS), c * 128 : (c + 1) * 128]
                cosb[level, pl.ds(r, ROWS), c * 128 : (c + 1) * 128] = jnp.take_along_axis(cos_tab, idx, axis=1, mode="promise_in_bounds")
                sinb[level, pl.ds(r, ROWS), c * 128 : (c + 1) * 128] = jnp.take_along_axis(sin_tab, idx, axis=1, mode="promise_in_bounds")

        rows_loop(body)

    def put_x(r, h, re, im):
        cols = slice(h * L, (h + 1) * L)
        for part, val in ((0, re), (1, im)):
            hi, lo = split(val)
            hl[pl.ds(part * L + r, ROWS), cols] = hi
            hl[pl.ds((2 + part) * L + r, ROWS), cols] = lo
            hl[pl.ds((4 + part) * L + r, ROWS), cols] = hi

    def slot(kind, f, k):
        if kind == 0:
            return gxb.at[f, k, a]
        if kind == 1:
            return gyb.at[f, k, b]
        return ccb.at[f, k, a, pl.ds(b, 1)]

    def arrivals(kind, f, k):
        block = (
            gxb.at[f, k, pl.ds(0, nx - 1)],
            gyb.at[f, k, pl.ds(0, ny - 1)],
            ccb.at[f, k, pl.ds(0, nx - 1), pl.ds(0, ny - 1)],
            ccb.at[f, k, pl.ds(0, nx - 1), pl.ds(0, 1)],
            ccb.at[f, k, 0, pl.ds(0, ny - 1)],
        )[kind]
        return pltpu.make_async_remote_copy(block, block, send_sem.at[kind, f, k], recv_sem.at[kind, f, k], device_id={"gx": a}, device_id_type=MESH)

    real8 = ((iota((8, L), 0) >> 1) & 1) == 0
    lane8, row8 = iota((8, 128), 1), iota((8, 128), 0)
    corner_mask = (((row8 >> 1) & 1) == 0) & ((lane8 >> 6) == (row8 & 1)) & (((lane8 >> 2) & 1) == (row8 >> 2)) & (((lane8 >> 3) & 7) == b)

    def times_i(q):
        return jnp.where(real8, -pltpu.roll(q, 6, 0), pltpu.roll(q, 2, 0))

    def local(f):
        w_ref[...] = mm(va[...], hl[...])

        def body(r):
            for h in (0, 1):
                for part in (0, 1):
                    hi, lo = split(w_ref[pl.ds(part * L + r, ROWS), h * L : (h + 1) * L])
                    hly[pl.ds(h * L + r, ROWS), part * L : (part + 1) * L] = hi
                    hly[pl.ds(h * L + r, ROWS), (2 + part) * L : (3 + part) * L] = lo
                    hly[pl.ds(h * L + r, ROWS), (4 + part) * L : (5 + part) * L] = hi

        rows_loop(body)
        u_ref[f] = mm(hly[...], vb[...])

    def carry(f, k):
        acc_x = acc_y = jnp.zeros((16, L), F32)
        for h in (0, 1):
            cols = slice(h * L, (h + 1) * L)
            acc_x = acc_x + mm(vl[h], hl[0 : 4 * L, cols])
            for i in range(4):
                acc_y = acc_y + mm_nt(vl[h, :, i * L : (i + 1) * L], hl[i * L : (i + 1) * L, cols])
        carries = jnp.concatenate([acc_x[0:8] + acc_x[8:16], acc_y[0:8] + acc_y[8:16]], axis=0)
        hi = carries.astype(BF16).astype(F32)
        both = jnp.concatenate([hi, carries - hi], axis=0).astype(BF16)
        out = mm(both, kw[0])
        out = out[0:16] + out[16:32] + mm(both[0:16], kw[1])
        gxb[f, k, a] = out[0:8, 0:L] + times_i(out[0:8, L : 2 * L])
        gyb[f, k, b] = out[8:16, 0:L] + times_i(out[8:16, L : 2 * L])
        corner = out[0:8, 2 * L : 2 * L + 128] + pltpu.roll(out[0:8, 2 * L + 128 : 3 * L], 6, 0)
        ccb[f, k, a, pl.ds(b, 1)] = jnp.sum(jnp.where(corner_mask, corner, 0.0), axis=0, keepdims=True)
    def send(f, k):
        for _, kind, peer in peers:
            here = slot(kind, f, k)
            pltpu.make_async_remote_copy(here, here, send_sem.at[kind, f, k], recv_sem.at[kind, f, k], device_id=peer, device_id_type=MESH).start()

    def start(f, k):
        carry(f, k)
        send(f, k)
        pl.when(a < nx)(lambda: local(f))

    def finish(f, k):
        for kind in range(5):
            arrivals(kind, f, k).wait_recv()
        pairs = nx // 2
        m = jnp.sum(ccb[f, k], axis=1, keepdims=True).reshape(pairs, 2, 1, 128)
        shape = (pairs, 8, 128)
        m = jnp.where(iota(shape, 1) < 4, jnp.broadcast_to(m[:, 0], shape), jnp.broadcast_to(m[:, 1], shape)).reshape(4 * nx, 128)
        left = iota((4 * nx, 128), 1) < 64
        row = iota((4 * nx, 128), 0)
        m = jnp.where((row & 1) == 1, pltpu.roll(m, 64, 1), m)
        hi = m.astype(BF16).astype(F32)
        m = jnp.concatenate([jnp.where(left, hi, pltpu.roll(m - hi, 64, 1)), jnp.where(left, hi, 0.0)], axis=1).astype(BF16)
        corr = mm(m, qc[...])
        real = ((iota((4 * nx, L), 0) >> 1) & 1) == 0
        g = gxb[f, k].reshape(pairs, 2, 8, L)
        even, odd = g[:, 0], g[:, 1]
        top = iota((pairs, 8, L), 1) < 4
        g = (jnp.where(top, even, pltpu.roll(odd, 4, 1)), jnp.where(top, pltpu.roll(even, 4, 1), odd))
        gx3 = []
        for h in (0, 1):
            val = g[h].reshape(4 * nx, L) + jnp.where(real, corr[:, 2 * h * L : (2 * h + 1) * L], corr[:, (2 * h + 1) * L : (2 * h + 2) * L])
            hi, lo = split(val)
            pad = jnp.zeros((64 - 4 * nx, L), BF16)
            fill = [pad] if 4 * nx < 64 else []
            gx3.append(jnp.concatenate([hi] + fill + [lo] + fill + [hi] + fill + [jnp.zeros((64, L), BF16)], axis=0))
        gy = gyb[f, k].reshape(8 * ny, L)
        hi = gy.astype(BF16).astype(F32)
        fill = [jnp.zeros((64 - 8 * ny, L), F32)] if 8 * ny < 64 else []
        gy3 = jnp.concatenate([hi] + fill + [gy - hi] + fill + [hi] + fill + [jnp.zeros((64, L), F32)], axis=0).T.astype(BF16)
        for h in (0, 1):
            for part in (0, 1):
                i = 2 * h + part
                xy[i * L : (i + 1) * L, :] = mm(qx[part], gx3[h]) + mm(gy3, qy[:, i * L : (i + 1) * L])

    def y_value(f, r, h):
        re = u_ref[f, pl.ds(h * L + r, ROWS), 0:L] + xy[pl.ds(2 * h * L + r, ROWS), :]
        im = u_ref[f, pl.ds(h * L + r, ROWS), L : 2 * L] + xy[pl.ds((2 * h + 1) * L + r, ROWS), :]
        return re, im

    def turn(level, r, h, re, im):
        cols = slice(h * L, (h + 1) * L)
        c = cosb[level, pl.ds(r, ROWS), cols]
        s = sinb[level, pl.ds(r, ROWS), cols]
        return re * c - im * s, re * s + im * c

    def source_turn(k):
        def body(r):
            for h in (0, 1):
                cols = slice(h * L, (h + 1) * L)
                re, im = turn(k, r, h, *y_value(0, r, h))
                slev[k + 1, pl.ds(r, ROWS), cols] = re
                slev[k + 1, pl.ds(L + r, ROWS), cols] = im
                put_x(r, h, re, im)

        rows_loop(body)

    def receiver_turn(k):
        level = jnp.maximum(DEPTH - 2 - k, 0)

        def body(r):
            for h in (0, 1):
                cols = slice(h * L, (h + 1) * L)
                re, im = y_value(1, r, h)
                rlev[DEPTH - 1 - k, pl.ds(r, ROWS), cols] = re
                rlev[DEPTH - 1 - k, pl.ds(L + r, ROWS), cols] = im
                put_x(r, h, *turn(level, r, h, re, im))

        rows_loop(body)

    def image(z):
        def body(r):
            img_o[z, pl.ds(r, ROWS), :] = (
                slev[z, pl.ds(r, ROWS), :] * rlev[z, pl.ds(r, ROWS), :]
                - slev[z, pl.ds(L + r, ROWS), :] * rlev[z, pl.ds(L + r, ROWS), :]
            )

        rows_loop(body)

    ins[0].wait()

    def first_source(r):
        for h in (0, 1):
            cols = slice(h * L, (h + 1) * L)
            put_x(r, h, slev[0, pl.ds(r, ROWS), cols], slev[0, pl.ds(L + r, ROWS), cols])

    rows_loop(first_source)
    carry(0, 0)
    ins[2].wait()
    for level in (DEPTH - 1, 0):
        look_up(level)
    ins[1].wait()
    pl.semaphore_wait(barrier, nx * ny - 1)
    send(0, 0)
    local(0)

    def first_receiver(r):
        for h in (0, 1):
            cols = slice(h * L, (h + 1) * L)
            put_x(r, h, *turn(DEPTH - 1, r, h, rin[pl.ds(r, ROWS), cols], -rin[pl.ds(L + r, ROWS), cols]))

    rows_loop(first_receiver)
    start(1, 0)
    for level in range(DEPTH - 2, 0, -1):
        look_up(level)

    def step(k, state):
        pl.when(a < nx)(lambda: finish(0, k))
        source_turn(k)
        start(0, k + 1)
        pl.when(a < nx)(lambda: finish(1, k))
        receiver_turn(k)
        start(1, k + 1)

        return state

    lax.fori_loop(0, DEPTH - 1, step, 0)

    def last_source(r):
        for h in (0, 1):
            cols = slice(h * L, (h + 1) * L)
            re, im = turn(DEPTH - 1, r, h, *y_value(0, r, h))
            bot_o[pl.ds(r, ROWS), cols] = re
            bot_o[pl.ds(L + r, ROWS), cols] = im

    def last_receiver(r):
        for h in (0, 1):
            cols = slice(h * L, (h + 1) * L)
            re, im = y_value(1, r, h)
            top_o[pl.ds(r, ROWS), cols] = re
            top_o[pl.ds(L + r, ROWS), cols] = -im
            img_o[0, pl.ds(r, ROWS), cols] = slev[0, pl.ds(r, ROWS), cols] * re - slev[0, pl.ds(L + r, ROWS), cols] * im

    for z in range(DEPTH - 1, 0, -1):
        image(z)
    finish(0, DEPTH - 1)
    rows_loop(last_source)
    finish(1, DEPTH - 1)
    rows_loop(last_receiver)
    for f in (0, 1):
        for k in range(DEPTH):
            for kind in range(5):
                arrivals(kind, f, k).wait_send()


def write_out(image, bottom, top, image_o, bottom_o, top_o, sem):
    copies = [pltpu.make_async_copy(v, o, sem.at[i]) for i, (v, o) in enumerate(((image, image_o), (bottom, bottom_o), (top, top_o)))]
    for copy in copies:
        copy.start()
    for copy in copies:
        copy.wait()


def solution(mesh):
    nx, ny = mesh.shape["gx"], mesh.shape["gy"]

    def on_device(source_field, receiver_field, velocity_index, slowness, freq_index, root_modulus, root_angle):
        width = source_field.shape[3]
        any_spec = pl.BlockSpec(memory_space=pl.ANY)
        hbm = pl.BlockSpec(memory_space=pltpu.HBM)
        smem = pl.BlockSpec(memory_space=pltpu.SMEM)
        image, bottom, top = pl.pallas_call(
            functools.partial(kernel, nx, ny),
            out_shape=(
                jax.ShapeDtypeStruct((DEPTH, L, width), F32),
                jax.ShapeDtypeStruct((2 * L, width), F32),
                jax.ShapeDtypeStruct((2 * L, width), F32),
            ),
            in_specs=[hbm] * 4 + [smem] * 3,
            out_specs=(pl.BlockSpec(memory_space=pltpu.VMEM),) * 3,
            scratch_shapes=[
                pltpu.VMEM((DEPTH, 2 * L, width), F32),
                pltpu.VMEM((DEPTH, 2 * L, width), F32),
                pltpu.VMEM((2 * L, width), F32),
                pltpu.VMEM((DEPTH, L, width), jnp.int32),
                pltpu.VMEM((DEPTH, L, width), F32),
                pltpu.VMEM((DEPTH, L, width), F32),
                pltpu.VMEM((8, 128), F32),
                pltpu.VMEM((2, 2 * L, width), F32),
                pltpu.VMEM((2 * L, width), F32),
                pltpu.VMEM((6 * L, width), BF16),
                pltpu.VMEM((2 * L, 6 * L), BF16),
                pltpu.VMEM((4 * L, L), F32),
                pltpu.VMEM((2 * L, 6 * L), BF16),
                pltpu.VMEM((6 * L, 2 * L), BF16),
                pltpu.VMEM((2, 16, 4 * L), BF16),
                pltpu.VMEM((2, L, 3 * L), BF16),
                pltpu.VMEM((2, L, L), BF16),
                pltpu.VMEM((L, 4 * L), BF16),
                pltpu.VMEM((L, 4 * L), BF16),
                pltpu.VMEM((2, DEPTH, nx, 8, L), F32),
                pltpu.VMEM((2, DEPTH, ny, 8, L), F32),
                pltpu.VMEM((2, DEPTH, nx, 8, 128), F32),
                pltpu.VMEM((1, 64), F32),
                pltpu.SemaphoreType.DMA((4,)),
                pltpu.SemaphoreType.DMA((5, 2, DEPTH)),
                pltpu.SemaphoreType.DMA((5, 2, DEPTH)),
            ],
            compiler_params=pltpu.CompilerParams(collective_id=0, has_side_effects=True, vmem_limit_bytes=44 * 2**20),
        )(
            pltpu.with_memory_space_constraint(source_field.reshape(2 * L, width), pltpu.HBM),
            pltpu.with_memory_space_constraint(receiver_field.reshape(2 * L, width), pltpu.HBM),
            pltpu.with_memory_space_constraint(velocity_index, pltpu.HBM),
            pltpu.with_memory_space_constraint(slowness.reshape(1, -1), pltpu.HBM),
            freq_index,
            root_modulus,
            root_angle,
        )
        image, bottom, top = pl.pallas_call(
            write_out,
            out_shape=tuple(jax.ShapeDtypeStruct(v.shape, F32) for v in (image, bottom, top)),
            in_specs=[any_spec] * 3,
            out_specs=(any_spec,) * 3,
            scratch_shapes=[pltpu.SemaphoreType.DMA((3,))],
            compiler_params=pltpu.CompilerParams(vmem_limit_bytes=2**20),
        )(image, bottom, top)
        return image, bottom.reshape(source_field.shape), top.reshape(receiver_field.shape)

    wave = P(None, None, "gx", "gy")
    return jax.shard_map(
        on_device,
        mesh=mesh,
        in_specs=(wave, wave, P(None, "gx", "gy"), P(), P(), P(), P()),
        out_specs=(P(None, "gx", "gy"), wave, wave),
        check_vma=False,
    )
```
